256 devices in a mesh: edge: 64 (over x, z, core), feat: 4 (over y).
Axes of the slice: x: 4, y: 4, z: 8, core: 2. Of those that a mesh axis runs over, the one named last changes fastest.
Arguments:
- node_feat: bfloat16 [131072, 128], P('edge'), may hold values from -6 to 6
- cotangent: bfloat16 [131072, 128], P('edge'), may hold values from -6 to 6
- w_msg: bfloat16 [128, 128], replicated, may hold values from -0.5 to 0.5
- w_self: bfloat16 [128, 128], replicated, may hold values from -0.5 to 0.5
- adjacency: bfloat16 [64, 4, 64, 128, 128], P('edge', 'feat'), may hold values from -0.125 to 0.125
- edge_src: int32 [64, 4, 64], P('edge', 'feat'), may hold values from 0 to 127
- edge_dst: int32 [64, 4, 64], P('edge', 'feat'), may hold values from 0 to 127
- send_src: int32 [64, 4, 64, 2], P('edge', 'feat'), may hold values from 0 to 15
- recv_dst: int32 [64, 4, 64, 2], P('edge', 'feat'), may hold values from 0 to 15
- live: int32 [64, 4], P('edge', 'feat'), may hold values from 4 to 64, as said below
Outputs:
- out_feat: bfloat16 [131072, 128], P('edge')
- grad_feat: bfloat16 [131072, 128], P('edge')
- grad_wmsg: float32 [128, 128], replicated
- grad_wself: float32 [128, 128], replicated
The draws below stay inside these ranges and needn't reach their ends.
Inputs may be any that keep to these rules, and one draw needn't show every extreme that they name: Each device has between 64 // 16 (at least 1) and 64 live blocks; one device always has all 64 live.
All inputs are finite; a program needn't handle non-finite values.
Results may differ from the reference program's by a relative error of at most 0.0054.
Values may be sent and summed in bfloat16 or wider, within the bound.
A program may use at most 128 MiB of HBM per device.

```python
import jax
import jax.numpy as jnp
from jax import lax

H = 128
BLK = 128
NB_DEV = 16
EB_DEV = 64
CAPS = 2
CAPD = 2
NODES = 131072
N_EDGE = 64
N_FEAT = 4


def draw_live(key, part):
    base = jax.random.randint(key, (N_EDGE * N_FEAT,), max(1, EB_DEV // 16), EB_DEV + 1)
    chosen = jax.random.randint(jax.random.fold_in(key, 7), (), 0, N_EDGE * N_FEAT)
    filled = jnp.where(jnp.arange(N_EDGE * N_FEAT, dtype=jnp.int32) == chosen, EB_DEV, base)
    return filled.reshape(N_EDGE, N_FEAT).astype(jnp.int32)


def with_ends(entries, own_key, least, top_value):
    shape = entries.shape
    spot = [jax.random.randint(jax.random.fold_in(own_key, axis), (), 0, shape[axis]) for axis in range(len(shape))]
    entries = entries.at[tuple(spot)].set(least)
    longest = shape.index(max(shape))
    spot[longest] = (spot[longest] + 1) % shape[longest]
    return entries.at[tuple(spot)].set(top_value)


def shard_levels(key, extent, pieces, smallest, high):
    loudness = 1.0
    for axis_at, parts in pieces:
        heights = jax.random.uniform(jax.random.fold_in(jax.random.fold_in(key, 6), axis_at), (parts,), jnp.float32, smallest / len(pieces), high / len(pieces))
        loudness = loudness * jnp.repeat(jnp.exp(heights), extent[axis_at] // parts).reshape((-1,) + (1,) * (len(extent) - 1 - axis_at))
    return loudness


def bell_draw(stream_key, dims, scale, most, shards=(), held_as=jnp.bfloat16):
    values = jax.random.normal(stream_key, dims, jnp.float32) * scale
    if len(shards) > 0:
        values = shard_levels(stream_key, dims, shards, -0.22, 0.18) * values
    return jnp.clip(values, min=-most, max=most).astype(held_as)


def setup_inputs(seed: int = 0) -> dict:
    splits = jax.random.split(jax.random.key(seed), 11)
    node_feat = bell_draw(splits[0], (NODES, H), 1.0, 6.0, ((0, 64),))
    cotangent = bell_draw(splits[1], (NODES, H), 1.0, 6.0, ((0, 64),))
    w_msg = bell_draw(splits[2], (H, H), H ** -0.5, 0.5)
    w_self = bell_draw(splits[3], (H, H), H ** -0.5, 0.5)
    adjacency = bell_draw(splits[4], (N_EDGE, N_FEAT, EB_DEV, BLK, BLK), (BLK * EB_DEV * N_FEAT // NB_DEV) ** -0.5, 0.125, ((0, 64), (1, 4)))
    edge_src = with_ends(jax.random.randint(splits[5], (N_EDGE, N_FEAT, EB_DEV), 0, N_EDGE * CAPS), jax.random.fold_in(splits[5], 1), 0, (N_EDGE * CAPS) - 1).astype(jnp.int32)
    edge_dst = with_ends(jax.random.randint(splits[6], (N_EDGE, N_FEAT, EB_DEV), 0, N_EDGE * CAPD), jax.random.fold_in(splits[6], 1), 0, (N_EDGE * CAPD) - 1).astype(jnp.int32)
    send_src = with_ends(jax.random.randint(splits[7], (N_EDGE, N_FEAT, N_EDGE, CAPS), 0, NB_DEV), jax.random.fold_in(splits[7], 1), 0, NB_DEV - 1).astype(jnp.int32)
    recv_dst = with_ends(jax.random.randint(splits[8], (N_EDGE, N_FEAT, N_EDGE, CAPD), 0, NB_DEV), jax.random.fold_in(splits[8], 1), 0, NB_DEV - 1).astype(jnp.int32)
    live = draw_live(jax.random.fold_in(splits[10], 71), 0)
    return dict(node_feat=node_feat, cotangent=cotangent, w_msg=w_msg, w_self=w_self, adjacency=adjacency, edge_src=edge_src, edge_dst=edge_dst, send_src=send_src, recv_dst=recv_dst, live=live)


def reference(node_feat, cotangent, w_msg, w_self, adjacency, edge_src, edge_dst, send_src, recv_dst, live):
    block_total = NB_DEV * N_EDGE
    device_total = N_EDGE * N_FEAT
    feat_index = jnp.arange(N_FEAT, dtype=jnp.int32)[None, :, None]
    edge_index = jnp.arange(N_EDGE, dtype=jnp.int32)[:, None, None]
    src_peer = edge_src // CAPS
    src_glob = src_peer * NB_DEV + send_src[src_peer, feat_index, edge_index, edge_src % CAPS]
    dst_owner = edge_dst // CAPD
    dst_glob = dst_owner * NB_DEV + recv_dst[dst_owner, feat_index, edge_index, edge_dst % CAPD]
    keep_mask = (jnp.arange(EB_DEV, dtype=jnp.int32)[None, None, :] < live[:, :, None]).astype(jnp.float32)
    blocks_all = adjacency.reshape(device_total, EB_DEV, BLK, BLK)
    src_flat = src_glob.reshape(device_total, EB_DEV).astype(jnp.int32)
    dst_flat = dst_glob.reshape(device_total, EB_DEV).astype(jnp.int32)
    keep_flat = keep_mask.reshape(device_total, EB_DEV)

    messages = jnp.dot(node_feat, w_msg, preferred_element_type=jnp.float32).astype(jnp.bfloat16)
    message_blocks = messages.reshape(block_total, BLK, H)

    def forward_step(running, scan_item):
        blocks, src_ids, dst_ids, keep_rows = scan_item
        terms = jnp.einsum("eij,ejh->eih", blocks.astype(jnp.float32), message_blocks[src_ids].astype(jnp.float32))
        terms = terms * keep_rows[:, None, None]
        return running.at[dst_ids].add(terms), None

    aggregate, _ = lax.scan(forward_step, jnp.zeros((block_total, BLK, H), jnp.float32), (blocks_all, src_flat, dst_flat, keep_flat))
    preact = jnp.dot(node_feat, w_self, preferred_element_type=jnp.float32) + aggregate.reshape(-1, H)
    sigmoid_pre = jax.nn.sigmoid(preact)
    out_feat = (preact * sigmoid_pre).astype(jnp.bfloat16)
    grad_pre = (cotangent.astype(jnp.float32) * sigmoid_pre * (1.0 + preact * (1.0 - sigmoid_pre))).astype(jnp.bfloat16)
    grad_wself = jnp.dot(node_feat.T, grad_pre, preferred_element_type=jnp.float32)
    grad_blocks = grad_pre.reshape(block_total, BLK, H)

    def backward_step(running, scan_item):
        blocks, src_ids, dst_ids, keep_rows = scan_item
        terms = jnp.einsum("eij,eih->ejh", blocks.astype(jnp.float32), grad_blocks[dst_ids].astype(jnp.float32))
        terms = terms * keep_rows[:, None, None]
        return running.at[src_ids].add(terms), None

    grad_sum, _ = lax.scan(backward_step, jnp.zeros((block_total, BLK, H), jnp.float32), (blocks_all, src_flat, dst_flat, keep_flat))
    grad_msg = grad_sum.reshape(-1, H).astype(jnp.bfloat16)
    grad_wmsg = jnp.dot(node_feat.T, grad_msg, preferred_element_type=jnp.float32)
    grad_feat = (jnp.dot(grad_pre, w_self.T, preferred_element_type=jnp.float32) + jnp.dot(grad_msg, w_msg.T, preferred_element_type=jnp.float32)).astype(jnp.bfloat16)
    return out_feat, grad_feat, grad_wmsg, grad_wself
```

```python
import jax
import jax.numpy as jnp
from jax import lax
from jax.experimental import pallas as pl
from jax.experimental.pallas import tpu as pltpu
from jax.sharding import PartitionSpec as P

MESH = pl.DeviceIdType.MESH
NX, NY, NZ = 4, 4, 8
BLK = 128
OWN = 16
QTR = OWN // NY
PEERS = 2 * NX
VMEM_LIMIT = 60 * 1024 * 1024
BF16, F32, I32 = jnp.bfloat16, jnp.float32, jnp.int32


def place():
    edge = lax.axis_index("edge")
    y = lax.axis_index("feat")
    return edge // 16, y, (edge // 2) % NZ, edge % 2


def device(x, y, z, c):
    return ((x * NZ + z) * 2 + c, y)


def zoff(k):
    return ((2 * (k % 2) - 1) * ((k + 1) // 2) + NZ) % NZ


def greet(peers):
    barrier = pltpu.get_barrier_semaphore()
    for peer in peers:
        pl.semaphore_signal(barrier, inc=1, device_id=peer, device_id_type=MESH)
    pl.semaphore_wait(barrier, len(peers))


def remote(src, dst, send, recv, peer):
    return pltpu.make_async_remote_copy(
        src_ref=src, dst_ref=dst, send_sem=send, recv_sem=recv, device_id=peer, device_id_type=MESH
    )


def slab_peer(x, c, j):
    return (x + j // 2) % NX, (c + j) % 2


def slab_source(x, c, j):
    return (x + NX - j // 2) % NX, (c + j) % 2


def group_peers(x, y, z, c):
    peers = [device(x, y, (z + d) % NZ, c) for d in range(1, NZ)]
    peers += [device(x, (y + d) % NY, z, c) for d in range(1, NY)]
    for j in range(1, PEERS):
        px, pc = slab_peer(x, c, j)
        peers.append(device(px, y, z, pc))
    return peers


def gather_kernel(tab, q_ref, r_ref, dense, chunk, staged, ls, zs, zr, ys, yr, xs, xr):
    x, y, z, c = place()
    me = x * 2 + c
    greet(group_peers(x, y, z, c))

    def zcopy(d):
        return remote(
            q_ref, dense.at[z, pl.ds(QTR * y, QTR)], zs.at[d], zr.at[d],
            device(x, y, (z + d) % NZ, c),
        )

    def ycopy(k, zi, d):
        quarter = dense.at[zi, pl.ds(QTR * y, QTR)]
        return remote(quarter, quarter, ys.at[k, d], yr.at[k, d], device(x, (y + d) % NY, z, c))

    def xcopy(k, zi, j):
        px, pc = slab_peer(x, c, j)
        return remote(
            staged.at[px * 2 + pc, zi], r_ref.at[me, zi], xs.at[k, j], xr.at[k, j],
            device(px, y, z, pc),
        )

    def spread(k):
        d = zoff(k)
        zi = (z + NZ - d) % NZ

        @pl.when(k > 0)
        def _():
            remote(
                q_ref, dense.at[zi, pl.ds(QTR * y, QTR)], zs.at[d], zr.at[d],
                device(x, y, (z + d) % NZ, c),
            ).wait_recv()

        for dy in (1, 3, 2):
            ycopy(k, zi, dy).start()

    def deliver(k):
        zi = (z + NZ - zoff(k)) % NZ
        for dy in (1, 3, 2):
            part = dense.at[zi, pl.ds(QTR * ((y + NY - dy) % NY), QTR)]
            remote(part, part, ys.at[k, dy], yr.at[k, dy], device(x, y, z, c)).wait_recv()

        chunk[...] = dense[zi]

        def pick(j, carry):
            px, pc = slab_peer(x, c, j)
            pid = px * 2 + pc
            for s in range(2):
                staged[pid, zi, s] = chunk[tab[(zi * PEERS + pid) * 2 + s]]
            return carry

        lax.fori_loop(1, PEERS, pick, 0)
        for s in range(2):
            r_ref[me, zi, s] = chunk[tab[(zi * PEERS + me) * 2 + s]]

        def push(j, carry):
            xcopy(k, zi, j).start()
            return carry

        lax.fori_loop(1, PEERS, push, 0)

    own = pltpu.make_async_copy(q_ref, dense.at[z, pl.ds(QTR * y, QTR)], ls)
    own.start()
    for d in (1, 7, 2, 6, 3, 5, 4):
        zcopy(d).start()
    own.wait()
    spread(0)
    spread(1)

    def step(k, carry):
        @pl.when(k < NZ - 2)
        def _():
            spread(k + 2)

        deliver(k)
        return carry

    lax.fori_loop(0, NZ, step, 0)

    for d in range(1, NZ):
        zcopy(d).wait_send()

    def finish(k, carry):
        zi = (z + NZ - zoff(k)) % NZ
        for dy in range(1, NY):
            ycopy(k, zi, dy).wait_send()

        def each(j, carry):
            xcopy(k, zi, j).wait_send()
            sx, sc = slab_source(x, c, j)
            remote(
                staged.at[me, zi], r_ref.at[sx * 2 + sc, zi], xs.at[k, j], xr.at[k, j],
                device(sx, y, z, sc),
            ).wait_recv()
            return carry

        lax.fori_loop(1, PEERS, each, 0)
        return carry

    lax.fori_loop(0, NZ, finish, 0)


def gather_blocks(tab, quarter):
    dma = pltpu.SemaphoreType.DMA
    return pl.pallas_call(
        gather_kernel,
        name="gather_blocks",
        out_shape=jax.ShapeDtypeStruct((PEERS, NZ, 2, BLK, BLK), BF16),
        in_specs=[
            pl.BlockSpec(memory_space=pltpu.SMEM),
            pl.BlockSpec(memory_space=pltpu.VMEM),
        ],
        out_specs=pl.BlockSpec(memory_space=pltpu.VMEM),
        scratch_shapes=[
            pltpu.VMEM((NZ, OWN, BLK, BLK), BF16),
            pltpu.VMEM((OWN, BLK, BLK), BF16),
            pltpu.VMEM((PEERS, NZ, 2, BLK, BLK), BF16),
            dma,
            dma((NZ,)),
            dma((NZ,)),
            dma((NZ, NY)),
            dma((NZ, NY)),
            dma((NZ, PEERS)),
            dma((NZ, PEERS)),
        ],
        compiler_params=pltpu.CompilerParams(
            collective_id=0, has_side_effects=True, vmem_limit_bytes=VMEM_LIMIT
        ),
    )(tab, quarter)


def scatter_kernel(
    order, keep, last, has, p_ref, o_ref,
    arrived, chunk, runs, ysend, yown, yrecv, zsend, zrecv, ls, xs, xr, ys, yr, zs, zr,
):
    x, y, z, c = place()
    me = x * 2 + c
    greet(group_peers(x, y, z, c))

    def owner(k):
        return (z + zoff(NZ - 1 - k)) % NZ

    def xcopy(k, j):
        zi = owner(k)
        px, pc = slab_peer(x, c, j)
        return remote(
            p_ref.at[px * 2 + pc, zi], arrived.at[zi, pl.ds(2 * me, 2)], xs.at[k, j], xr.at[k, j],
            device(px, y, z, pc),
        )

    def local(k):
        zi = owner(k)
        return pltpu.make_async_copy(p_ref.at[me, zi], arrived.at[zi, pl.ds(2 * me, 2)], ls.at[k])

    def ycopy(k, d):
        return remote(
            ysend.at[k, d - 1], yrecv.at[k, d - 1], ys.at[k, d], yr.at[k, d],
            device(x, (y + d) % NY, z, c),
        )

    def zcopy(d):
        return remote(
            zsend.at[d - 1], zrecv.at[d - 1], zs.at[d], zr.at[d], device(x, y, (z + d) % NZ, c)
        )

    def push(k, carry):
        local(k).start()

        def each(j, carry):
            xcopy(k, j).start()
            return carry

        return lax.fori_loop(1, PEERS, each, carry)

    lax.fori_loop(0, NZ, push, 0)

    def merge(k):
        zi = owner(k)
        local(k).wait()

        def each(j, carry):
            sx, sc = slab_source(x, c, j)
            remote(
                p_ref.at[me, zi], arrived.at[zi, pl.ds(2 * (sx * 2 + sc), 2)],
                xs.at[k, j], xr.at[k, j], device(sx, y, z, sc),
            ).wait_recv()
            return carry

        lax.fori_loop(1, PEERS, each, 0)

        chunk[...] = arrived[zi]

        def run(i, total):
            at = zi * OWN + i
            total = total * keep[at] + chunk[order[at]].astype(F32)
            runs[i] = total
            return total

        lax.fori_loop(0, OWN, run, jnp.zeros((BLK, BLK), F32))
        for d in (1, 3, 2):
            base = zi * OWN + QTR * ((y + d) % NY)
            for b in range(QTR):
                ysend[k, d - 1, b] = (runs[last[base + b]] * has[base + b]).astype(BF16)
            ycopy(k, d).start()
        base = zi * OWN + QTR * y
        for b in range(QTR):
            yown[k, b] = runs[last[base + b]] * has[base + b]

    def total_of(k):
        for d in range(1, NY):
            ycopy(k, d).wait_recv()
        return [
            yown[k, b] + yrecv[k, 0, b].astype(F32) + yrecv[k, 1, b].astype(F32)
            + yrecv[k, 2, b].astype(F32)
            for b in range(QTR)
        ]

    def forward(k):
        d = zoff(NZ - 1 - k)
        for b, value in enumerate(total_of(k)):
            zsend[d - 1, b] = value.astype(BF16)
        zcopy(d).start()

    merge(0)

    def step(k, carry):
        merge(k)
        forward(k - 1)
        return carry

    lax.fori_loop(1, NZ, step, 0)
    for b, value in enumerate(total_of(NZ - 1)):
        o_ref[b] = value
    for d in (1, 7, 2, 6, 3, 5, 4):
        zcopy(d).wait_recv()
        for b in range(QTR):
            o_ref[b] += zrecv[d - 1, b].astype(F32)

    for d in range(1, NZ):
        zcopy(d).wait_send()

    def finish(k, carry):
        for d in range(1, NY):
            ycopy(k, d).wait_send()

        def each(j, carry):
            xcopy(k, j).wait_send()
            return carry

        return lax.fori_loop(1, PEERS, each, carry)

    lax.fori_loop(0, NZ, finish, 0)


def scatter_blocks(tables, partials):
    dma = pltpu.SemaphoreType.DMA
    smem = pl.BlockSpec(memory_space=pltpu.SMEM)
    return pl.pallas_call(
        scatter_kernel,
        name="scatter_blocks",
        out_shape=jax.ShapeDtypeStruct((QTR, BLK, BLK), F32),
        in_specs=[smem, smem, smem, smem, pl.BlockSpec(memory_space=pltpu.VMEM)],
        out_specs=pl.BlockSpec(memory_space=pltpu.VMEM),
        scratch_shapes=[
            pltpu.VMEM((NZ, OWN, BLK, BLK), BF16),
            pltpu.VMEM((OWN, BLK, BLK), BF16),
            pltpu.VMEM((OWN, BLK, BLK), F32),
            pltpu.VMEM((NZ, NY - 1, QTR, BLK, BLK), BF16),
            pltpu.VMEM((NZ, QTR, BLK, BLK), F32),
            pltpu.VMEM((NZ, NY - 1, QTR, BLK, BLK), BF16),
            pltpu.VMEM((NZ - 1, QTR, BLK, BLK), BF16),
            pltpu.VMEM((NZ - 1, QTR, BLK, BLK), BF16),
            dma((NZ,)),
            dma((NZ, PEERS)),
            dma((NZ, PEERS)),
            dma((NZ, NY)),
            dma((NZ, NY)),
            dma((NZ,)),
            dma((NZ,)),
        ],
        compiler_params=pltpu.CompilerParams(
            collective_id=1, has_side_effects=True, vmem_limit_bytes=VMEM_LIMIT
        ),
    )(*tables, partials)


GROUP = 8


def edge_kernel(forward, rounds, pick, put, adj_ref, rows_ref, o_ref, total):
    slots = rows_ref.shape[0]

    def clear(i, carry):
        total[i] = jnp.zeros((BLK, BLK), F32)
        return carry

    lax.fori_loop(0, slots, clear, 0)
    contract = (((1,), (0,)), ((), ())) if forward else (((0,), (0,)), ((), ()))

    def one_round(r, carry):
        terms = []
        for i in range(GROUP):
            k = r * GROUP + i
            terms.append(
                lax.dot_general(adj_ref[k], rows_ref[pick[k]], contract, preferred_element_type=F32)
            )
        for i in range(GROUP):
            at = put[r * GROUP + i]
            total[at] += terms[i]
        return carry

    lax.fori_loop(0, rounds[0], one_round, 0)

    def write(i, carry):
        o_ref[i] = total[i].astype(BF16)
        return carry

    lax.fori_loop(0, slots, write, 0)


def edge_terms(forward, rounds, pick, put, adj, rows):
    slots = rows.shape[0]
    smem = pl.BlockSpec(memory_space=pltpu.SMEM)
    vmem = pl.BlockSpec(memory_space=pltpu.VMEM)

    def run(*refs):
        edge_kernel(forward, *refs)

    return pl.pallas_call(
        run,
        name="edge_forward" if forward else "edge_backward",
        out_shape=jax.ShapeDtypeStruct(rows.shape, BF16),
        in_specs=[smem, smem, smem, vmem, vmem],
        out_specs=vmem,
        scratch_shapes=[pltpu.VMEM((slots + 1, BLK, BLK), F32)],
        compiler_params=pltpu.CompilerParams(vmem_limit_bytes=VMEM_LIMIT),
    )(rounds, pick, put, adj, rows)


SLAB = NX * NY * 2


def slab_device(x, y, z, c, j):
    return device((x + j // (2 * NY)) % NX, (y + (j // 2) % NY) % NY, z, (c + j) % 2)


def final_kernel(w_ref, a_ref, b_ref, oa_ref, ob_ref, ow_ref, first, mine, second, ls, gs, gr, s1, r1, s2, r2, s3, r3):
    x, y, z, c = place()
    me = (x * NY + y) * 2 + c
    rows = w_ref.shape[0] // SLAB
    height = a_ref.shape[0]

    def index(j):
        return (((x + j // (2 * NY)) % NX) * NY + (y + (j // 2) % NY) % NY) * 2 + (c + j) % 2

    def source(j):
        return (
            ((x + NX - j // (2 * NY)) % NX) * NY + (y + NY - (j // 2) % NY) % NY
        ) * 2 + (c + j) % 2

    peers = [slab_device(x, y, z, c, j) for j in range(1, SLAB)]
    peers += [device(x, y, (z + d) % NZ, c) for d in range(1, NZ)]
    greet(peers)

    def one(j):
        return remote(
            w_ref.at[pl.ds(rows * index(j), rows)], first.at[me], s1.at[j], r1.at[j],
            slab_device(x, y, z, c, j),
        )

    def two(d):
        return remote(mine.at[0], second.at[z], s2.at[d], r2.at[d], device(x, y, (z + d) % NZ, c))

    def three(j):
        return remote(
            mine.at[1], ow_ref.at[pl.ds(rows * me, rows)], s3.at[j], r3.at[j],
            slab_device(x, y, z, c, j),
        )

    def spread(i, d):
        src, dst = ((a_ref, oa_ref), (b_ref, ob_ref))[i]
        return remote(
            src, dst.at[pl.ds(height * y, height)], gs.at[i, d], gr.at[i, d],
            device(x, (y + d) % NY, z, c),
        )

    def loop(body):
        def run(j, carry):
            body(j)
            return carry

        lax.fori_loop(1, SLAB, run, 0)

    loop(lambda j: one(j).start())
    first[me] = w_ref[pl.ds(rows * me, rows)]
    locals_ = [
        pltpu.make_async_copy(src, dst.at[pl.ds(height * y, height)], ls.at[i])
        for i, (src, dst) in enumerate(((a_ref, oa_ref), (b_ref, ob_ref)))
    ]
    for i in (0, 1):
        locals_[i].start()
        for d in (1, 3, 2):
            spread(i, d).start()

    def arrived(j):
        remote(
            w_ref.at[pl.ds(0, rows)], first.at[source(j)], s1.at[j], r1.at[j], device(x, y, z, c)
        ).wait_recv()

    loop(arrived)
    mine[0] = jnp.sum(first[...], axis=0)
    for d in range(1, NZ):
        two(d).start()
    second[z] = mine[0]
    for d in range(1, NZ):
        remote(
            mine.at[0], second.at[(z + NZ - d) % NZ], s2.at[d], r2.at[d], device(x, y, z, c)
        ).wait_recv()
    mine[1] = jnp.sum(second[...], axis=0)
    loop(lambda j: three(j).start())
    ow_ref[pl.ds(rows * me, rows)] = mine[1]

    def landed(j):
        remote(
            mine.at[1], ow_ref.at[pl.ds(rows * source(j), rows)], s3.at[j], r3.at[j],
            device(x, y, z, c),
        ).wait_recv()

    loop(landed)
    loop(lambda j: one(j).wait_send())
    for d in range(1, NZ):
        two(d).wait_send()
    loop(lambda j: three(j).wait_send())
    for i in (0, 1):
        locals_[i].wait()
        for d in range(1, NY):
            spread(i, d).wait_send()
            src, dst = ((a_ref, oa_ref), (b_ref, ob_ref))[i]
            remote(
                src, dst.at[pl.ds(height * ((y + NY - d) % NY), height)], gs.at[i, d], gr.at[i, d],
                device(x, y, z, c),
            ).wait_recv()


def finish(weights, a, b):
    dma = pltpu.SemaphoreType.DMA
    vmem = pl.BlockSpec(memory_space=pltpu.VMEM)
    rows, height, hidden = weights.shape[0] // SLAB, a.shape[0], a.shape[1]
    return pl.pallas_call(
        final_kernel,
        name="finish",
        out_shape=(
            jax.ShapeDtypeStruct((NY * height, hidden), BF16),
            jax.ShapeDtypeStruct((NY * height, hidden), BF16),
            jax.ShapeDtypeStruct(weights.shape, F32),
        ),
        in_specs=[vmem, vmem, vmem],
        out_specs=(vmem, vmem, vmem),
        scratch_shapes=[
            pltpu.VMEM((SLAB, rows, hidden), F32),
            pltpu.VMEM((2, rows, hidden), F32),
            pltpu.VMEM((NZ, rows, hidden), F32),
            dma((2,)),
            dma((2, NY)),
            dma((2, NY)),
            dma((SLAB,)),
            dma((SLAB,)),
            dma((NZ,)),
            dma((NZ,)),
            dma((SLAB,)),
            dma((SLAB,)),
        ],
        compiler_params=pltpu.CompilerParams(
            collective_id=2, has_side_effects=True, vmem_limit_bytes=VMEM_LIMIT
        ),
    )(weights, a, b)


def slot_index(slot):
    x, z, c, s = slot // 32, (slot // 4) % NZ, (slot // 2) % 2, slot % 2
    return ((x * 2 + c) * NZ + z) * 2 + s


def run_tables(blocks):
    n = blocks.shape[1]
    at = jnp.arange(n, dtype=I32)
    mine, other = blocks[:, :, None], blocks[:, None, :]
    ahead = (other < mine) | ((other == mine) & (at[None, None, :] < at[None, :, None]))
    rank = jnp.sum(ahead.astype(I32), axis=2)
    hit = rank[:, :, None] == at[None, None, :]
    order = jnp.sum(jnp.where(hit, at[None, :, None], 0), axis=1)
    first = jnp.sum((other == mine) & (at[None, None, :] < at[None, :, None]), axis=2) == 0
    keep = jnp.sum(jnp.where(hit & ~first[:, :, None], 1.0, 0.0), axis=1)
    upto = jnp.sum((blocks[:, None, :] <= at[None, :, None]).astype(I32), axis=2)
    has = jnp.any(blocks[:, None, :] == at[None, :, None], axis=2)
    return (
        order.reshape(-1),
        keep.astype(F32).reshape(-1),
        jnp.maximum(upto - 1, 0).reshape(-1),
        has.astype(F32).reshape(-1),
    )


def relay_tables(send_src, recv_dst):
    both = jnp.concatenate([send_src.reshape(NX, NZ, 2, 2), recv_dst.reshape(NX, NZ, 2, 2)], axis=3)
    both = both.transpose(1, 0, 2, 3).reshape(NZ, PEERS * 4)
    groups = [[(x * NZ + z) * 2 + c for z in range(NZ)] for x in range(NX) for c in range(2)]
    both = lax.all_to_all(
        both, "edge", split_axis=0, concat_axis=0, axis_index_groups=groups, tiled=True
    ).reshape(NZ, PEERS, 4)
    return both[:, :, :2].reshape(NZ, OWN), both[:, :, 2:].reshape(NZ, OWN)


def body(
    node_feat, cotangent, w_msg, w_self, adjacency, edge_src, edge_dst, send_src, recv_dst, live
):
    hidden = node_feat.shape[1]
    quarter = node_feat.shape[0] // NY
    plane = lax.axis_index("feat")
    nodes = lax.dynamic_slice_in_dim(node_feat, plane * quarter, quarter, 0)
    cot = lax.dynamic_slice_in_dim(cotangent, plane * quarter, quarter, 0)

    src_blocks, dst_blocks = relay_tables(send_src, recv_dst)
    adj = adjacency.reshape(-1, BLK, BLK)
    edges = adj.shape[0]
    alive = jnp.arange(edges, dtype=I32) < live.reshape(())
    rounds = ((live.reshape(1) + GROUP - 1) // GROUP).astype(I32)
    src_slot = slot_index(edge_src.reshape(-1))
    dst_slot = slot_index(edge_dst.reshape(-1))
    slots = PEERS * NZ * 2

    def gather(blocks, rows):
        got = gather_blocks(blocks.reshape(-1), rows.reshape(QTR, BLK, hidden))
        return got.reshape(slots, BLK, hidden)

    def scatter(blocks, parts):
        total = scatter_blocks(run_tables(blocks), parts.reshape(PEERS, NZ, 2, BLK, hidden))
        return total.reshape(quarter, hidden)

    messages = jnp.dot(nodes, w_msg, preferred_element_type=F32).astype(BF16)
    incoming = gather(src_blocks, messages)
    parts = edge_terms(True, rounds, src_slot, jnp.where(alive, dst_slot, slots), adj, incoming)
    aggregate = scatter(dst_blocks, parts)
    preact = jnp.dot(nodes, w_self, preferred_element_type=F32) + aggregate
    sig = jax.nn.sigmoid(preact)
    out = (preact * sig).astype(BF16)
    grad_pre = (cot.astype(F32) * sig * (1.0 + preact * (1.0 - sig))).astype(BF16)
    rows_of = (((0,), (0,)), ((), ()))
    wself = lax.dot_general(nodes, grad_pre, rows_of, preferred_element_type=F32)
    grad_in = gather(dst_blocks, grad_pre)
    grad_parts = edge_terms(False, rounds, dst_slot, jnp.where(alive, src_slot, slots), adj, grad_in)
    grad_msg = scatter(src_blocks, grad_parts).astype(BF16)
    wmsg = lax.dot_general(nodes, grad_msg, rows_of, preferred_element_type=F32)
    grad_feat = (
        jnp.dot(grad_pre, w_self.T, preferred_element_type=F32)
        + jnp.dot(grad_msg, w_msg.T, preferred_element_type=F32)
    ).astype(BF16)
    out, grad_feat, weights = finish(jnp.concatenate([wmsg, wself], axis=0), out, grad_feat)
    return out, grad_feat, weights[:hidden], weights[hidden:]


def solution(mesh):
    in_specs = (
        P("edge", None),
        P("edge", None),
        P(),
        P(),
        P("edge", "feat", None, None, None),
        P("edge", "feat", None),
        P("edge", "feat", None),
        P("edge", "feat", None, None),
        P("edge", "feat", None, None),
        P("edge", "feat"),
    )
    out_specs = (P("edge", None), P("edge", None), P(), P())
    return jax.shard_map(body, mesh=mesh, in_specs=in_specs, out_specs=out_specs, check_vma=False)
```

```python
import jax
import jax.numpy as jnp
from jax import lax
from jax.experimental import pallas as pl
from jax.experimental.pallas import tpu as pltpu
from jax.sharding import PartitionSpec as P

MESH = pl.DeviceIdType.MESH
NX, NY, NZ = 4, 4, 8
BLK = 128
OWN = 16
QTR = OWN // NY
PEERS = 2 * NX
VMEM_LIMIT = 60 * 1024 * 1024
GROUP = 8
SLAB = NX * NY * 2
CHUNK = 2 * PEERS
EDGES = 64
SLOTS = 128
SRC, SRC_PREV, SRC_LAST, DST, DST_PREV, DST_LAST = range(6)
BF16, F32, I32 = jnp.bfloat16, jnp.float32, jnp.int32


def place():
    edge = lax.axis_index("edge")
    y = lax.axis_index("feat")
    return edge // 16, y, (edge // 2) % NZ, edge % 2


def device(x, y, z, c):
    return ((x * NZ + z) * 2 + c, y)


def zoff(k):
    return ((2 * (k % 2) - 1) * ((k + 1) // 2) + NZ) % NZ


def remote(src, dst, send, recv, peer):
    return pltpu.make_async_remote_copy(
        src_ref=src, dst_ref=dst, send_sem=send, recv_sem=recv, device_id=peer, device_id_type=MESH
    )


def slab_peer(x, c, j):
    return (x + j // 2) % NX, (c + j) % 2


def slab_source(x, c, j):
    return (x + NX - j // 2) % NX, (c + j) % 2


def slab_device(x, y, z, c, j):
    return device((x + j // (2 * NY)) % NX, (y + (j // 2) % NY) % NY, z, (c + j) % 2)


def loop(first, stop, body):
    def run(i, carry):
        body(i)
        return carry

    lax.fori_loop(first, stop, run, 0)


def dot(a, b, contract):
    return lax.dot_general(a, b, (contract, ((), ())), preferred_element_type=F32)


def tables_kernel(blocks_ref, edges_ref, meta_ref, etab_ref):
    shape = blocks_ref.shape
    blocks = blocks_ref[...]
    lane = lax.broadcasted_iota(I32, shape, 1)
    prev = jnp.full(shape, CHUNK, I32)
    for d in range(CHUNK - 1, 0, -1):
        same = (pltpu.roll(blocks, d, 1) == blocks) & (lane >= d) & (lane < CHUNK)
        prev = jnp.where(same, lane - d, prev)
    last = jnp.full(shape, CHUNK, I32)
    for i in range(CHUNK):
        last = jnp.where(blocks[:, i : i + 1] == lane, i, last)
    for row, (value, at) in enumerate(
        ((blocks, 0), (prev, 0), (last, 0), (blocks, NZ), (prev, NZ), (last, NZ))
    ):
        for z in range(NZ):
            meta_ref[z, row : row + 1] = value[at + z : at + z + 1]

    wide = (SLOTS, SLOTS)
    down = lax.broadcasted_iota(I32, wide, 0)
    along = lax.broadcasted_iota(I32, wide, 1)
    downf, alongf = down.astype(F32), along.astype(F32)
    live = edges_ref[2:3, :]
    none = float(EDGES)
    for row, prev_row, last_row in ((0, SRC_PREV, SRC_LAST), (1, DST_PREV, DST_LAST)):
        slot = edges_ref[row : row + 1, :]
        etab_ref[(SRC, DST)[row] : (SRC, DST)[row] + 1] = slot
        on = lax.broadcasted_iota(I32, slot.shape, 1) < live
        flat = jnp.where(on, slot.astype(F32), -1.0)
        tall = jnp.sum(jnp.where(down == along, flat, 0.0), axis=1, keepdims=True)
        before = jnp.where((tall == flat) & (down < along) & (tall >= 0.0), downf, -1.0)
        found = jnp.max(before, axis=0, keepdims=True)
        etab_ref[prev_row : prev_row + 1] = jnp.where(found < 0.0, none, found).astype(I32)
        ends = jnp.max(jnp.where(tall == alongf, downf, -1.0), axis=0, keepdims=True)
        etab_ref[last_row : last_row + 1] = jnp.where(ends < 0.0, none, ends).astype(I32)


def tables(blocks, edges):
    return pl.pallas_call(
        tables_kernel,
        name="tables",
        out_shape=(
            jax.ShapeDtypeStruct((NZ, 8, SLOTS), I32),
            jax.ShapeDtypeStruct((8, SLOTS), I32),
        ),
    )(blocks, edges)


def layer_kernel(
    etab, meta_ref, nf_ref, cot_ref, wm_ref, ws_ref, adj_ref,
    out_ref, gf_ref, ow_ref,
    meta_in, meta, adj, dense, chunk, staged, rows, chain, parts, arrived, runs,
    ysend, yown, yrecv, zsend, zrecv, total, pre, weights, first, mine, second,
    al, ml, ms, mr, g_zs, g_zr, g_ys, g_yr, g_xs, g_xr,
    ls, s_xs, s_xr, s_ys, s_yr, s_zs, s_zr, gs, gr, s1, r1, s2, r2, s3, r3,
):
    x, y, z, c = place()
    me = x * 2 + c
    quarter = QTR * BLK
    here = device(x, y, z, c)
    mine_rows = pl.ds(quarter * y, quarter)
    own = pl.ds(QTR * y, QTR)

    barrier = pltpu.get_barrier_semaphore()
    peers = [slab_device(x, y, z, c, j) for j in range(1, SLAB)]
    peers += [device(x, y, (z + d) % NZ, c) for d in range(1, NZ)]
    for peer in peers:
        pl.semaphore_signal(barrier, inc=1, device_id=peer, device_id_type=MESH)

    adj_copy = pltpu.make_async_copy(adj_ref, adj, al)
    adj_copy.start()
    own_meta = pltpu.make_async_copy(meta_ref.at[z], meta.at[z], ml.at[0])
    own_meta.start()

    def project(i):
        b = (QTR * y + i) % OWN
        node = nf_ref[pl.ds(pl.multiple_of(b * BLK, BLK), BLK)]
        dense[z, b] = dot(node, wm_ref[...], ((1,), (0,))).astype(BF16)

    loop(0, OWN, project)
    pl.semaphore_wait(barrier, len(peers))

    def slots_of(px, zi, pc):
        return pl.ds(((px * NZ + zi) * 2 + pc) * 2, 2)

    def gather(forward):
        block_row = SRC if forward else DST

        def mcopy(d):
            return remote(
                meta_ref.at[(z + d) % NZ], meta_in.at[z], ms.at[d], mr.at[d],
                device(x, y, (z + d) % NZ, c),
            )

        def zcopy(d):
            part = dense.at[z, own]
            return remote(part, part, g_zs.at[d], g_zr.at[d], device(x, y, (z + d) % NZ, c))

        def ycopy(k, zi, d):
            part = dense.at[zi, own]
            return remote(part, part, g_ys.at[k, d], g_yr.at[k, d], device(x, (y + d) % NY, z, c))

        def xcopy(k, zi, j):
            px, pc = slab_peer(x, c, j)
            return remote(
                staged.at[px * 2 + pc, zi], rows.at[slots_of(x, zi, c)], g_xs.at[k, j], g_xr.at[k, j],
                device(px, y, z, pc),
            )

        def meta_load(k, zi):
            return pltpu.make_async_copy(meta_in.at[zi], meta.at[zi], ml.at[k])

        def spread(k):
            d = zoff(k)
            zi = (z + NZ - d) % NZ
            part = dense.at[zi, own]
            if forward:
                remote(meta_ref.at[z], meta_in.at[zi], ms.at[d], mr.at[d], here).wait_recv()
                meta_load(k, zi).start()
            remote(part, part, g_zs.at[d], g_zr.at[d], here).wait_recv()
            for dy in (1, 3, 2):
                ycopy(k, zi, dy).start()

        def collect(k):
            zi = (z + NZ - zoff(k)) % NZ
            for dy in (1, 3, 2):
                part = dense.at[zi, pl.ds(QTR * ((y + NY - dy) % NY), QTR)]
                remote(part, part, g_ys.at[k, dy], g_yr.at[k, dy], here).wait_recv()
            if forward:
                meta_load(k, zi).wait()

        def deliver(k):
            zi = (z + NZ - zoff(k)) % NZ
            chunk[...] = dense[zi]

            def pick(j):
                px, pc = slab_peer(x, c, j)
                pid = px * 2 + pc
                for s in range(2):
                    staged[pid, zi, s] = chunk[meta[zi, block_row, pid * 2 + s]]

            loop(1, PEERS, pick)
            base = ((x * NZ + zi) * 2 + c) * 2
            for s in range(2):
                rows[base + s] = chunk[meta[zi, block_row, me * 2 + s]]
            loop(1, PEERS, lambda j: xcopy(k, zi, j).start())

        for d in (1, 7, 2, 6, 3, 5, 4):
            if forward:
                mcopy(d).start()
            zcopy(d).start()
        if forward:
            own_meta.wait()
            deliver(0)
            spread(1)
        else:
            for dy in (1, 3, 2):
                ycopy(0, z, dy).start()
            spread(1)
            collect(0)
            deliver(0)

        def step(k):
            @pl.when(k < NZ - 1)
            def _():
                spread(k + 1)

            collect(k)
            deliver(k)

        loop(1, NZ, step)

        for d in range(1, NZ):
            if forward:
                mcopy(d).wait_send()
            zcopy(d).wait_send()

        def finish(k):
            zi = (z + NZ - zoff(k)) % NZ

            def each(j):
                xcopy(k, zi, j).wait_send()
                sx, sc = slab_source(x, c, j)
                remote(
                    staged.at[me, zi], rows.at[slots_of(sx, zi, sc)], g_xs.at[k, j], g_xr.at[k, j], here
                ).wait_recv()

            loop(1, PEERS, each)

        loop(0, NZ, finish)

        def sent(k):
            zi = (z + NZ - zoff(k)) % NZ
            for dy in range(1, NY):
                ycopy(k, zi, dy).wait_send()

        loop(1 if forward else 0, NZ, sent)

    def edges(forward):
        pick, prev = (SRC, DST_PREV) if forward else (DST, SRC_PREV)
        contract = ((1,), (0,)) if forward else ((0,), (0,))
        chain[EDGES] = jnp.zeros((BLK, BLK), F32)

        def one_round(r):
            terms = []
            for i in range(GROUP):
                k = r * GROUP + i
                terms.append(dot(adj[k], rows[etab[pick, k]], contract))
            for i in range(GROUP):
                k = r * GROUP + i
                chain[k] = terms[i] + chain[etab[prev, k]]

        loop(0, EDGES // GROUP, one_round)

    def scatter(forward):
        end = DST_LAST if forward else SRC_LAST
        run_prev, run_last = (DST_PREV, DST_LAST) if forward else (SRC_PREV, SRC_LAST)

        def owner(k):
            return (z + zoff(NZ - 1 - k)) % NZ

        def xcopy(k, j):
            zi = owner(k)
            px, pc = slab_peer(x, c, j)
            return remote(
                parts.at[slots_of(px, zi, pc)], arrived.at[zi, pl.ds(2 * me, 2)],
                s_xs.at[k, j], s_xr.at[k, j], device(px, y, z, pc),
            )

        def local(k):
            zi = owner(k)
            return pltpu.make_async_copy(
                parts.at[slots_of(x, zi, c)], arrived.at[zi, pl.ds(2 * me, 2)], ls.at[k]
            )

        def ycopy(k, d):
            return remote(
                ysend.at[k, d - 1], yrecv.at[k, d - 1], s_ys.at[k, d], s_yr.at[k, d],
                device(x, (y + d) % NY, z, c),
            )

        def zcopy(d):
            return remote(
                zsend.at[d - 1], zrecv.at[d - 1], s_zs.at[d], s_zr.at[d], device(x, y, (z + d) % NZ, c)
            )

        def write(k):
            zi = owner(k)

            def each(pid):
                base = (((pid // 2) * NZ + zi) * 2 + pid % 2) * 2
                for s in range(2):
                    parts[base + s] = chain[etab[end, base + s]].astype(BF16)

            loop(0, PEERS, each)

        def push(k):
            local(k).start()
            loop(1, PEERS, lambda j: xcopy(k, j).start())

        write(0)

        def issue(k):
            write(k)
            push(k - 1)

        loop(1, NZ, issue)
        push(NZ - 1)

        runs[CHUNK] = jnp.zeros((BLK, BLK), F32)

        def merge(k):
            zi = owner(k)
            local(k).wait()

            def each(j):
                sx, sc = slab_source(x, c, j)
                remote(
                    parts.at[slots_of(x, zi, c)], arrived.at[zi, pl.ds(2 * (sx * 2 + sc), 2)],
                    s_xs.at[k, j], s_xr.at[k, j], here,
                ).wait_recv()

            loop(1, PEERS, each)

            def run(i):
                runs[i] = arrived[zi, i].astype(F32) + runs[meta[zi, run_prev, i]]

            loop(0, CHUNK, run)
            for d in (1, 3, 2):
                base = QTR * ((y + d) % NY)
                for b in range(QTR):
                    ysend[k, d - 1, b] = runs[meta[zi, run_last, base + b]].astype(BF16)
                ycopy(k, d).start()
            for b in range(QTR):
                yown[k, b] = runs[meta[zi, run_last, QTR * y + b]]

        def total_of(k):
            for d in range(1, NY):
                ycopy(k, d).wait_recv()
            return [
                yown[k, b] + yrecv[k, 0, b].astype(F32) + yrecv[k, 1, b].astype(F32)
                + yrecv[k, 2, b].astype(F32)
                for b in range(QTR)
            ]

        def pass_on(k):
            d = zoff(NZ - 1 - k)
            for b, value in enumerate(total_of(k)):
                zsend[d - 1, b] = value.astype(BF16)
            zcopy(d).start()

        merge(0)

        def step(k):
            merge(k)
            pass_on(k - 1)

        loop(1, NZ, step)
        for b, value in enumerate(total_of(NZ - 1)):
            total[b] = value
        for d in (1, 7, 2, 6, 3, 5, 4):
            zcopy(d).wait_recv()
            for b in range(QTR):
                total[b] += zrecv[d - 1, b].astype(F32)

        for d in range(1, NZ):
            zcopy(d).wait_send()

        def finish(k):
            for d in range(1, NY):
                ycopy(k, d).wait_send()
            loop(1, PEERS, lambda j: xcopy(k, j).wait_send())

        loop(0, NZ, finish)

    def share(i, d):
        part = (out_ref, gf_ref)[i].at[mine_rows]
        return remote(part, part, gs.at[i, d], gr.at[i, d], device(x, (y + d) % NY, z, c))

    def shared(i):
        for d in range(1, NY):
            share(i, d).wait_send()
            part = (out_ref, gf_ref)[i].at[pl.ds(quarter * ((y + NY - d) % NY), quarter)]
            remote(part, part, gs.at[i, d], gr.at[i, d], here).wait_recv()

    def block_rows(b):
        return pl.ds(pl.multiple_of((QTR * y + b) * BLK, BLK), BLK)

    gather(True)
    adj_copy.wait()
    edges(True)
    scatter(True)

    def activate(b):
        node = nf_ref[block_rows(b)]
        preact = dot(node, ws_ref[...], ((1,), (0,))) + total[b]
        sig = jax.nn.sigmoid(preact)
        out_ref[block_rows(b)] = (preact * sig).astype(BF16)
        grad = cot_ref[block_rows(b)].astype(F32) * sig * (1.0 + preact * (1.0 - sig))
        grad = grad.astype(BF16)
        pre[b] = grad
        dense[z, QTR * y + b] = grad

    def outer(at, b, value):
        term = dot(nf_ref[block_rows(b)], value, ((0,), (0,)))
        if b == 0:
            weights[at : at + BLK] = term
        else:
            weights[at : at + BLK] += term

    for b in range(QTR):
        activate(b)
    for b in range(QTR):
        outer(BLK, b, pre[b])

    gather(False)
    edges(False)
    for d in (1, 3, 2):
        share(0, d).start()
    scatter(False)

    for b in range(QTR):
        outer(0, b, total[b].astype(BF16))

    height = 2 * BLK // SLAB
    slab_me = (x * NY + y) * 2 + c

    def index(j):
        return (((x + j // (2 * NY)) % NX) * NY + (y + (j // 2) % NY) % NY) * 2 + (c + j) % 2

    def source(j):
        return (
            ((x + NX - j // (2 * NY)) % NX) * NY + (y + NY - (j // 2) % NY) % NY
        ) * 2 + (c + j) % 2

    def one(j):
        return remote(
            weights.at[pl.ds(height * index(j), height)], first.at[slab_me], s1.at[j], r1.at[j],
            slab_device(x, y, z, c, j),
        )

    def two(d):
        return remote(mine.at[0], second.at[z], s2.at[d], r2.at[d], device(x, y, (z + d) % NZ, c))

    def three(j):
        return remote(
            mine.at[1], ow_ref.at[pl.ds(height * slab_me, height)], s3.at[j], r3.at[j],
            slab_device(x, y, z, c, j),
        )

    loop(1, SLAB, lambda j: one(j).start())
    first[slab_me] = weights[pl.ds(height * slab_me, height)]
    for b in range(QTR):
        gf_ref[block_rows(b)] = (
            dot(pre[b], ws_ref[...], ((1,), (1,)))
            + dot(total[b].astype(BF16), wm_ref[...], ((1,), (1,)))
        ).astype(BF16)
    for d in (1, 3, 2):
        share(1, d).start()
    loop(
        1, SLAB,
        lambda j: remote(
            weights.at[pl.ds(0, height)], first.at[source(j)], s1.at[j], r1.at[j], here
        ).wait_recv(),
    )
    mine[0] = jnp.sum(first[...], axis=0)
    for d in range(1, NZ):
        two(d).start()
    second[z] = mine[0]
    for d in range(1, NZ):
        remote(mine.at[0], second.at[(z + NZ - d) % NZ], s2.at[d], r2.at[d], here).wait_recv()
    mine[1] = jnp.sum(second[...], axis=0)
    loop(1, SLAB, lambda j: three(j).start())
    ow_ref[pl.ds(height * slab_me, height)] = mine[1]
    loop(
        1, SLAB,
        lambda j: remote(
            mine.at[1], ow_ref.at[pl.ds(height * source(j), height)], s3.at[j], r3.at[j], here
        ).wait_recv(),
    )
    loop(1, SLAB, lambda j: one(j).wait_send())
    for d in range(1, NZ):
        two(d).wait_send()
    loop(1, SLAB, lambda j: three(j).wait_send())
    shared(0)
    shared(1)


def layer(etab, meta, nf, cot, wm, ws, adj):
    dma = pltpu.SemaphoreType.DMA
    vmem = pl.BlockSpec(memory_space=pltpu.VMEM)
    hidden = nf.shape[1]
    block = (BLK, hidden)
    height = 2 * BLK // SLAB
    return pl.pallas_call(
        layer_kernel,
        name="layer",
        out_shape=(
            jax.ShapeDtypeStruct(nf.shape, BF16),
            jax.ShapeDtypeStruct(nf.shape, BF16),
            jax.ShapeDtypeStruct((2 * hidden, hidden), F32),
        ),
        in_specs=[pl.BlockSpec(memory_space=pltpu.SMEM), vmem, vmem, vmem, vmem, vmem, pl.BlockSpec(memory_space=pl.ANY)],
        out_specs=(vmem, vmem, vmem),
        scratch_shapes=[
            pltpu.VMEM((NZ, 8, SLOTS), I32),
            pltpu.SMEM((NZ, 8, SLOTS), I32),
            pltpu.VMEM((EDGES, BLK, BLK), BF16),
            pltpu.VMEM((NZ, OWN, *block), BF16),
            pltpu.VMEM((OWN, *block), BF16),
            pltpu.VMEM((PEERS, NZ, 2, *block), BF16),
            pltpu.VMEM((SLOTS, *block), BF16),
            pltpu.VMEM((EDGES + 1, *block), F32),
            pltpu.VMEM((SLOTS, *block), BF16),
            pltpu.VMEM((NZ, CHUNK, *block), BF16),
            pltpu.VMEM((CHUNK + 1, *block), F32),
            pltpu.VMEM((NZ, NY - 1, QTR, *block), BF16),
            pltpu.VMEM((NZ, QTR, *block), F32),
            pltpu.VMEM((NZ, NY - 1, QTR, *block), BF16),
            pltpu.VMEM((NZ - 1, QTR, *block), BF16),
            pltpu.VMEM((NZ - 1, QTR, *block), BF16),
            pltpu.VMEM((QTR, *block), F32),
            pltpu.VMEM((QTR, *block), BF16),
            pltpu.VMEM((2 * hidden, hidden), F32),
            pltpu.VMEM((SLAB, height, hidden), F32),
            pltpu.VMEM((2, height, hidden), F32),
            pltpu.VMEM((NZ, height, hidden), F32),
            dma,
            dma((NZ,)),
            dma((NZ,)),
            dma((NZ,)),
            dma((NZ,)),
            dma((NZ,)),
            dma((NZ, NY)),
            dma((NZ, NY)),
            dma((NZ, PEERS)),
            dma((NZ, PEERS)),
            dma((NZ,)),
            dma((NZ, PEERS)),
            dma((NZ, PEERS)),
            dma((NZ, NY)),
            dma((NZ, NY)),
            dma((NZ,)),
            dma((NZ,)),
            dma((2, NY)),
            dma((2, NY)),
            dma((SLAB,)),
            dma((SLAB,)),
            dma((NZ,)),
            dma((NZ,)),
            dma((SLAB,)),
            dma((SLAB,)),
        ],
        compiler_params=pltpu.CompilerParams(
            collective_id=0, has_side_effects=True, vmem_limit_bytes=VMEM_LIMIT
        ),
    )(etab, meta, nf, cot, wm, ws, adj)


def store_kernel(a_ref, b_ref, w_ref, oa_ref, ob_ref, om_ref, os_ref, sems):
    half = w_ref.shape[0] // 2
    copies = [
        pltpu.make_async_copy(src, dst, sems.at[i])
        for i, (src, dst) in enumerate(
            (
                (a_ref, oa_ref),
                (b_ref, ob_ref),
                (w_ref.at[pl.ds(0, half)], om_ref),
                (w_ref.at[pl.ds(half, half)], os_ref),
            )
        )
    ]
    for copy in copies:
        copy.start()
    for copy in copies:
        copy.wait()


def store(a, b, w):
    vmem = pl.BlockSpec(memory_space=pltpu.VMEM)
    hbm = pl.BlockSpec(memory_space=pl.ANY)
    piece = jax.ShapeDtypeStruct((w.shape[0] // 2, w.shape[1]), F32)
    return pl.pallas_call(
        store_kernel,
        name="store",
        out_shape=(
            jax.ShapeDtypeStruct(a.shape, a.dtype),
            jax.ShapeDtypeStruct(b.shape, b.dtype),
            piece,
            piece,
        ),
        in_specs=[vmem, vmem, vmem],
        out_specs=(hbm, hbm, hbm, hbm),
        scratch_shapes=[pltpu.SemaphoreType.DMA((4,))],
    )(a, b, w)


def by_slab(slots):
    rows = slots.reshape(NX, NZ, 2, 2).transpose(1, 0, 2, 3).reshape(NZ, CHUNK)
    return rows


def body(
    node_feat, cotangent, w_msg, w_self, adjacency, edge_src, edge_dst, send_src, recv_dst, live
):
    blocks = jnp.concatenate([by_slab(send_src), by_slab(recv_dst)], axis=0)
    blocks = jnp.pad(blocks, ((0, 0), (0, SLOTS - CHUNK)), constant_values=-1)
    slots = jnp.concatenate([edge_src.reshape(1, EDGES), edge_dst.reshape(1, EDGES)], axis=0)
    slots = jnp.pad(slots, ((0, 6), (0, SLOTS - EDGES)))
    row = lax.broadcasted_iota(I32, slots.shape, 0)
    slots = jnp.where(row == 2, live.reshape(1, 1), slots)
    meta, etab = tables(blocks, slots)
    adj = adjacency.reshape(-1, BLK, BLK)
    out, grad_feat, weights = layer(etab, meta, node_feat, cotangent, w_msg, w_self, adj)
    return store(out, grad_feat, weights)


def solution(mesh):
    in_specs = (
        P("edge", None),
        P("edge", None),
        P(),
        P(),
        P("edge", "feat", None, None, None),
        P("edge", "feat", None),
        P("edge", "feat", None),
        P("edge", "feat", None, None),
        P("edge", "feat", None, None),
        P("edge", "feat"),
    )
    out_specs = (P("edge", None), P("edge", None), P(), P())
    return jax.shard_map(body, mesh=mesh, in_specs=in_specs, out_specs=out_specs, check_vma=False)
```

```python
import jax
import jax.numpy as jnp
from jax import lax
from jax.experimental import pallas as pl
from jax.experimental.pallas import tpu as pltpu
from jax.sharding import PartitionSpec as P

MESH = pl.DeviceIdType.MESH
NX, NY, NZ = 4, 4, 8
BLK = 128
OWN = 16
QTR = OWN // NY
PEERS = 2 * NX
VMEM_LIMIT = 60 * 1024 * 1024
GROUP = 8
NH = 2
PIECE = BLK // NH
NT = NZ * NH
SLAB = NX * NY * 2
CHUNK = 2 * PEERS
EDGES = 64
SLOTS = 128
SRC, SRC_PREV, SRC_LAST, DST, DST_PREV, DST_LAST = range(6)
BF16, F32, I32 = jnp.bfloat16, jnp.float32, jnp.int32


def place():
    edge = lax.axis_index("edge")
    y = lax.axis_index("feat")
    return edge // 16, y, (edge // 2) % NZ, edge % 2


def device(x, y, z, c):
    return ((x * NZ + z) * 2 + c, y)


def zoff(k):
    return ((2 * (k % 2) - 1) * ((k + 1) // 2) + NZ) % NZ


def remote(src, dst, send, recv, peer):
    return pltpu.make_async_remote_copy(
        src_ref=src, dst_ref=dst, send_sem=send, recv_sem=recv, device_id=peer, device_id_type=MESH
    )


def slab_peer(x, c, j):
    return (x + j // 2) % NX, (c + j) % 2


def slab_source(x, c, j):
    return (x + NX - j // 2) % NX, (c + j) % 2


def slab_device(x, y, z, c, j):
    return device((x + j // (2 * NY)) % NX, (y + (j // 2) % NY) % NY, z, (c + j) % 2)


def loop(first, stop, body):
    def run(i, carry):
        body(i)
        return carry

    lax.fori_loop(first, stop, run, 0)


def dot(a, b, contract):
    return lax.dot_general(a, b, (contract, ((), ())), preferred_element_type=F32)


def tables_kernel(blocks_ref, edges_ref, meta_ref, etab_ref):
    shape = blocks_ref.shape
    blocks = blocks_ref[...]
    lane = lax.broadcasted_iota(I32, shape, 1)
    prev = jnp.full(shape, CHUNK, I32)
    for d in range(CHUNK - 1, 0, -1):
        same = (pltpu.roll(blocks, d, 1) == blocks) & (lane >= d) & (lane < CHUNK)
        prev = jnp.where(same, lane - d, prev)
    last = jnp.full(shape, CHUNK, I32)
    for i in range(CHUNK):
        last = jnp.where(blocks[:, i : i + 1] == lane, i, last)
    for row, (value, at) in enumerate(
        ((blocks, 0), (prev, 0), (last, 0), (blocks, NZ), (prev, NZ), (last, NZ))
    ):
        for z in range(NZ):
            meta_ref[z, row : row + 1] = value[at + z : at + z + 1]

    wide = (SLOTS, SLOTS)
    down = lax.broadcasted_iota(I32, wide, 0)
    along = lax.broadcasted_iota(I32, wide, 1)
    downf, alongf = down.astype(F32), along.astype(F32)
    live = edges_ref[2:3, :]
    none = float(EDGES)
    for row, prev_row, last_row in ((0, SRC_PREV, SRC_LAST), (1, DST_PREV, DST_LAST)):
        slot = edges_ref[row : row + 1, :]
        etab_ref[(SRC, DST)[row] : (SRC, DST)[row] + 1] = slot
        on = lax.broadcasted_iota(I32, slot.shape, 1) < live
        flat = jnp.where(on, slot.astype(F32), -1.0)
        tall = jnp.sum(jnp.where(down == along, flat, 0.0), axis=1, keepdims=True)
        before = jnp.where((tall == flat) & (down < along) & (tall >= 0.0), downf, -1.0)
        found = jnp.max(before, axis=0, keepdims=True)
        etab_ref[prev_row : prev_row + 1] = jnp.where(found < 0.0, none, found).astype(I32)
        ends = jnp.max(jnp.where(tall == alongf, downf, -1.0), axis=0, keepdims=True)
        etab_ref[last_row : last_row + 1] = jnp.where(ends < 0.0, none, ends).astype(I32)


def tables(blocks, edges):
    return pl.pallas_call(
        tables_kernel,
        name="tables",
        out_shape=(
            jax.ShapeDtypeStruct((NZ, 8, SLOTS), I32),
            jax.ShapeDtypeStruct((8, SLOTS), I32),
        ),
    )(blocks, edges)


def layer_kernel(
    etab, meta_ref, nf_ref, cot_ref, wm_ref, ws_ref, adj_ref,
    out_ref, gf_ref, ow_ref,
    meta_in, meta, adj, dense, chunk, staged, rows, chain, parts, arrived, runs,
    ysend, yown, yrecv, zsend, zrecv, total, pre, weights, first, mine, second,
    al, ml, ms, mr, g_zs, g_zr, g_ys, g_yr, g_xs, g_xr,
    ls, s_xs, s_xr, s_ys, s_yr, s_zs, s_zr, gs, gr, s1, r1, s2, r2, s3, r3,
):
    x, y, z, c = place()
    me = x * 2 + c
    quarter = QTR * BLK
    here = device(x, y, z, c)
    mine_rows = pl.ds(quarter * y, quarter)
    own = pl.ds(QTR * y, QTR)

    barrier = pltpu.get_barrier_semaphore()
    peers = [slab_device(x, y, z, c, j) for j in range(1, SLAB)]
    peers += [device(x, y, (z + d) % NZ, c) for d in range(1, NZ)]
    for peer in peers:
        pl.semaphore_signal(barrier, inc=1, device_id=peer, device_id_type=MESH)

    adj_copy = pltpu.make_async_copy(adj_ref, adj, al)
    adj_copy.start()
    own_meta = pltpu.make_async_copy(meta_ref.at[z], meta.at[z], ml.at[0])
    own_meta.start()

    def project(i):
        b = (QTR * y + i) % OWN
        node = nf_ref[pl.ds(pl.multiple_of(b * BLK, BLK), BLK)]
        message = dot(node, wm_ref[...], ((1,), (0,))).astype(BF16)
        for h in range(NH):
            dense[z, h, b] = message[h * PIECE : (h + 1) * PIECE]

    loop(0, OWN, project)
    pl.semaphore_wait(barrier, len(peers))

    def slots_of(px, zi, pc):
        return pl.ds(((px * NZ + zi) * 2 + pc) * 2, 2)

    def gather(forward):
        block_row = SRC if forward else DST

        def source_of(t):
            return (z + NZ - zoff(t // NH)) % NZ

        def mcopy(d):
            return remote(
                meta_ref.at[(z + d) % NZ], meta_in.at[z], ms.at[d], mr.at[d],
                device(x, y, (z + d) % NZ, c),
            )

        def zcopy(zi, h, d, step):
            part = dense.at[zi, h, own]
            at = d * NH + h
            return remote(part, part, g_zs.at[at], g_zr.at[at], device(x, y, (z + NZ + step) % NZ, c))

        def ycopy(t, d):
            part = dense.at[source_of(t), t % NH, own]
            return remote(part, part, g_ys.at[t, d], g_yr.at[t, d], device(x, (y + d) % NY, z, c))

        def xcopy(t, j):
            px, pc = slab_peer(x, c, j)
            zi = source_of(t)
            return remote(
                staged.at[px * 2 + pc, zi, t % NH], rows.at[slots_of(x, zi, c), t % NH],
                g_xs.at[t, j], g_xr.at[t, j], device(px, y, z, pc),
            )

        def meta_load(k, zi):
            return pltpu.make_async_copy(meta_in.at[zi], meta.at[zi], ml.at[k])

        def spread(t):
            k, h = t // NH, t % NH
            d = zoff(k)
            zi = source_of(t)
            if forward:

                @pl.when(h == 0)
                def _():
                    remote(meta_ref.at[z], meta_in.at[zi], ms.at[d], mr.at[d], here).wait_recv()
                    meta_load(k, zi).start()

            part = dense.at[zi, h, own]
            at = d * NH + h
            remote(part, part, g_zs.at[at], g_zr.at[at], here).wait_recv()

            @pl.when(k < NZ - 2)
            def _():
                step = 2 * (k % 2) - 1
                zcopy(zi, h, (d + NZ + step) % NZ, step).start()

            for dy in (1, 3, 2):
                ycopy(t, dy).start()

        def collect(t):
            zi = source_of(t)
            for dy in (1, 3, 2):
                part = dense.at[zi, t % NH, pl.ds(QTR * ((y + NY - dy) % NY), QTR)]
                remote(part, part, g_ys.at[t, dy], g_yr.at[t, dy], here).wait_recv()
            if forward:

                @pl.when(t % NH == 0)
                def _():
                    meta_load(t // NH, zi).wait()

        def deliver(t):
            zi, h = source_of(t), t % NH
            chunk[...] = dense[zi, h]

            def pick(j):
                px, pc = slab_peer(x, c, j)
                pid = px * 2 + pc
                for s in range(2):
                    staged[pid, zi, h, s] = chunk[meta[zi, block_row, pid * 2 + s]]

            loop(1, PEERS, pick)
            base = ((x * NZ + zi) * 2 + c) * 2
            for s in range(2):
                rows[base + s, h] = chunk[meta[zi, block_row, me * 2 + s]]
            loop(1, PEERS, lambda j: xcopy(t, j).start())

        for h in range(NH):
            for d, step in ((1, 1), (NZ - 1, -1)):
                zcopy(z, h, d, step).start()
        if forward:
            for d in (1, 7, 2, 6, 3, 5, 4):
                mcopy(d).start()
            own_meta.wait()
            loop(0, NH, deliver)
            loop(NH, 2 * NH, spread)
        else:
            for h in range(NH):
                for dy in (1, 3, 2):
                    ycopy(h, dy).start()

        def step(t):
            @pl.when(t < NH * (NZ - 1))
            def _():
                spread(t + NH)

            collect(t)
            deliver(t)

        loop(NH if forward else 0, NH * NZ, step)

        for d in range(1, NZ):
            if forward:
                mcopy(d).wait_send()
            for h in range(NH):
                zcopy(z, h, d, 1).wait_send()

        def finish(t):
            zi = source_of(t)

            def each(j):
                xcopy(t, j).wait_send()
                sx, sc = slab_source(x, c, j)
                remote(
                    staged.at[me, zi, t % NH], rows.at[slots_of(sx, zi, sc), t % NH],
                    g_xs.at[t, j], g_xr.at[t, j], here,
                ).wait_recv()

            loop(1, PEERS, each)

        loop(0, NH * NZ, finish)

        def sent(t):
            for dy in range(1, NY):
                ycopy(t, dy).wait_send()

        loop(NH if forward else 0, NH * NZ, sent)

    def whole(pieces):
        return pieces.reshape(BLK, pieces.shape[-1])

    def edges(forward):
        pick, prev = (SRC, DST_PREV) if forward else (DST, SRC_PREV)
        contract = ((1,), (0,)) if forward else ((0,), (0,))
        chain[EDGES] = jnp.zeros(chain.shape[1:], F32)

        def one_round(r):
            terms = []
            for i in range(GROUP):
                k = r * GROUP + i
                terms.append(dot(adj[k], whole(rows[etab[pick, k]]), contract))
            for i in range(GROUP):
                k = r * GROUP + i
                chain[k] = terms[i].reshape(chain.shape[1:]) + chain[etab[prev, k]]

        loop(0, EDGES // GROUP, one_round)

    def scatter(forward):
        end = DST_LAST if forward else SRC_LAST
        run_prev, run_last = (DST_PREV, DST_LAST) if forward else (SRC_PREV, SRC_LAST)

        def owner(t):
            return (z + zoff(NZ - 1 - t // NH)) % NZ

        def xcopy(t, j):
            zi, h = owner(t), t % NH
            px, pc = slab_peer(x, c, j)
            return remote(
                parts.at[slots_of(px, zi, pc), h], arrived.at[zi, h, pl.ds(2 * me, 2)],
                s_xs.at[t, j], s_xr.at[t, j], device(px, y, z, pc),
            )

        def local(t):
            zi, h = owner(t), t % NH
            return pltpu.make_async_copy(
                parts.at[slots_of(x, zi, c), h], arrived.at[zi, h, pl.ds(2 * me, 2)], ls.at[t]
            )

        def ycopy(t, d):
            return remote(
                ysend.at[t, d - 1], yrecv.at[t, d - 1], s_ys.at[t, d], s_yr.at[t, d],
                device(x, (y + d) % NY, z, c),
            )

        def zcopy(d, h):
            at = d * NH + h
            return remote(
                zsend.at[d - 1, h], zrecv.at[d - 1, h], s_zs.at[at], s_zr.at[at],
                device(x, y, (z + d) % NZ, c),
            )

        def write(t):
            zi, h = owner(t), t % NH

            def each(pid):
                base = (((pid // 2) * NZ + zi) * 2 + pid % 2) * 2
                for s in range(2):
                    parts[base + s, h] = chain[etab[end, base + s], h].astype(BF16)

            loop(0, PEERS, each)

        def push(t):
            local(t).start()
            loop(1, PEERS, lambda j: xcopy(t, j).start())

        write(0)

        def issue(t):
            write(t)
            push(t - 1)

        loop(1, NH * NZ, issue)
        push(NH * NZ - 1)

        runs[CHUNK] = jnp.zeros(runs.shape[1:], F32)

        def merge(t):
            zi, h = owner(t), t % NH
            local(t).wait()

            def each(j):
                sx, sc = slab_source(x, c, j)
                remote(
                    parts.at[slots_of(x, zi, c), h], arrived.at[zi, h, pl.ds(2 * (sx * 2 + sc), 2)],
                    s_xs.at[t, j], s_xr.at[t, j], here,
                ).wait_recv()

            loop(1, PEERS, each)

            def run(i):
                runs[i] = arrived[zi, h, i].astype(F32) + runs[meta[zi, run_prev, i]]

            loop(0, CHUNK, run)
            for d in (1, 3, 2):
                base = QTR * ((y + d) % NY)
                for b in range(QTR):
                    ysend[t, d - 1, b] = runs[meta[zi, run_last, base + b]].astype(BF16)
                ycopy(t, d).start()
            for b in range(QTR):
                yown[t, b] = runs[meta[zi, run_last, QTR * y + b]]

        def total_of(t):
            for d in range(1, NY):
                ycopy(t, d).wait_recv()
            return [
                yown[t, b] + yrecv[t, 0, b].astype(F32) + yrecv[t, 1, b].astype(F32)
                + yrecv[t, 2, b].astype(F32)
                for b in range(QTR)
            ]

        def pass_on(t):
            d, h = zoff(NZ - 1 - t // NH), t % NH
            for b, value in enumerate(total_of(t)):
                zsend[d - 1, h, b] = value.astype(BF16)
            zcopy(d, h).start()

        loop(0, NH, merge)

        def step(t):
            merge(t)
            pass_on(t - NH)

        loop(NH, NH * NZ, step)
        for h in range(NH):
            for b, value in enumerate(total_of(NH * (NZ - 1) + h)):
                total[b, h] = value
        for d in (1, 7, 2, 6, 3, 5, 4):
            for h in range(NH):
                zcopy(d, h).wait_recv()
                for b in range(QTR):
                    total[b, h] += zrecv[d - 1, h, b].astype(F32)

        for d in range(1, NZ):
            for h in range(NH):
                zcopy(d, h).wait_send()

        def finish(t):
            for d in range(1, NY):
                ycopy(t, d).wait_send()
            loop(1, PEERS, lambda j: xcopy(t, j).wait_send())

        loop(0, NH * NZ, finish)

    def share(i, d):
        part = (out_ref, gf_ref)[i].at[mine_rows]
        return remote(part, part, gs.at[i, d], gr.at[i, d], device(x, (y + d) % NY, z, c))

    def shared(i):
        for d in range(1, NY):
            share(i, d).wait_send()
            part = (out_ref, gf_ref)[i].at[pl.ds(quarter * ((y + NY - d) % NY), quarter)]
            remote(part, part, gs.at[i, d], gr.at[i, d], here).wait_recv()

    def block_rows(b):
        return pl.ds(pl.multiple_of((QTR * y + b) * BLK, BLK), BLK)

    gather(True)
    adj_copy.wait()
    edges(True)
    scatter(True)

    def activate(b):
        node = nf_ref[block_rows(b)]
        preact = dot(node, ws_ref[...], ((1,), (0,))) + whole(total[b])
        sig = jax.nn.sigmoid(preact)
        out_ref[block_rows(b)] = (preact * sig).astype(BF16)
        grad = cot_ref[block_rows(b)].astype(F32) * sig * (1.0 + preact * (1.0 - sig))
        grad = grad.astype(BF16)
        pre[b] = grad
        for h in range(NH):
            dense[z, h, QTR * y + b] = grad[h * PIECE : (h + 1) * PIECE]

    def outer(at, b, value):
        term = dot(nf_ref[block_rows(b)], value, ((0,), (0,)))
        if b == 0:
            weights[at : at + BLK] = term
        else:
            weights[at : at + BLK] += term

    for b in range(QTR):
        activate(b)
    for b in range(QTR):
        outer(BLK, b, pre[b])

    gather(False)
    edges(False)
    for d in (1, 3, 2):
        share(0, d).start()
    scatter(False)

    for b in range(QTR):
        outer(0, b, whole(total[b]).astype(BF16))

    height = 2 * BLK // SLAB
    slab_me = (x * NY + y) * 2 + c

    def index(j):
        return (((x + j // (2 * NY)) % NX) * NY + (y + (j // 2) % NY) % NY) * 2 + (c + j) % 2

    def source(j):
        return (
            ((x + NX - j // (2 * NY)) % NX) * NY + (y + NY - (j // 2) % NY) % NY
        ) * 2 + (c + j) % 2

    def one(j):
        return remote(
            weights.at[pl.ds(height * index(j), height)], first.at[slab_me], s1.at[j], r1.at[j],
            slab_device(x, y, z, c, j),
        )

    def two(d):
        return remote(mine.at[0], second.at[z], s2.at[d], r2.at[d], device(x, y, (z + d) % NZ, c))

    def three(j):
        return remote(
            mine.at[1], ow_ref.at[pl.ds(height * slab_me, height)], s3.at[j], r3.at[j],
            slab_device(x, y, z, c, j),
        )

    loop(1, SLAB, lambda j: one(j).start())
    first[slab_me] = weights[pl.ds(height * slab_me, height)]
    for b in range(QTR):
        gf_ref[block_rows(b)] = (
            dot(pre[b], ws_ref[...], ((1,), (1,)))
            + dot(whole(total[b]).astype(BF16), wm_ref[...], ((1,), (1,)))
        ).astype(BF16)
    for d in (1, 3, 2):
        share(1, d).start()
    loop(
        1, SLAB,
        lambda j: remote(
            weights.at[pl.ds(0, height)], first.at[source(j)], s1.at[j], r1.at[j], here
        ).wait_recv(),
    )
    mine[0] = jnp.sum(first[...], axis=0)
    for d in range(1, NZ):
        two(d).start()
    second[z] = mine[0]
    for d in range(1, NZ):
        remote(mine.at[0], second.at[(z + NZ - d) % NZ], s2.at[d], r2.at[d], here).wait_recv()
    mine[1] = jnp.sum(second[...], axis=0)
    loop(1, SLAB, lambda j: three(j).start())
    ow_ref[pl.ds(height * slab_me, height)] = mine[1]
    loop(
        1, SLAB,
        lambda j: remote(
            mine.at[1], ow_ref.at[pl.ds(height * source(j), height)], s3.at[j], r3.at[j], here
        ).wait_recv(),
    )
    loop(1, SLAB, lambda j: one(j).wait_send())
    for d in range(1, NZ):
        two(d).wait_send()
    loop(1, SLAB, lambda j: three(j).wait_send())
    shared(0)
    shared(1)


def layer(etab, meta, nf, cot, wm, ws, adj):
    dma = pltpu.SemaphoreType.DMA
    vmem = pl.BlockSpec(memory_space=pltpu.VMEM)
    hidden = nf.shape[1]
    block, piece = (BLK, hidden), (PIECE, hidden)
    height = 2 * BLK // SLAB
    return pl.pallas_call(
        layer_kernel,
        name="layer",
        out_shape=(
            jax.ShapeDtypeStruct(nf.shape, BF16),
            jax.ShapeDtypeStruct(nf.shape, BF16),
            jax.ShapeDtypeStruct((2 * hidden, hidden), F32),
        ),
        in_specs=[pl.BlockSpec(memory_space=pltpu.SMEM), vmem, vmem, vmem, vmem, vmem, pl.BlockSpec(memory_space=pl.ANY)],
        out_specs=(vmem, vmem, vmem),
        scratch_shapes=[
            pltpu.VMEM((NZ, 8, SLOTS), I32),
            pltpu.SMEM((NZ, 8, SLOTS), I32),
            pltpu.VMEM((EDGES, BLK, BLK), BF16),
            pltpu.VMEM((NZ, NH, OWN, *piece), BF16),
            pltpu.VMEM((OWN, *piece), BF16),
            pltpu.VMEM((PEERS, NZ, NH, 2, *piece), BF16),
            pltpu.VMEM((SLOTS, NH, *piece), BF16),
            pltpu.VMEM((EDGES + 1, NH, *piece), F32),
            pltpu.VMEM((SLOTS, NH, *piece), BF16),
            pltpu.VMEM((NZ, NH, CHUNK, *piece), BF16),
            pltpu.VMEM((CHUNK + 1, *piece), F32),
            pltpu.VMEM((NT, NY - 1, QTR, *piece), BF16),
            pltpu.VMEM((NT, QTR, *piece), F32),
            pltpu.VMEM((NT, NY - 1, QTR, *piece), BF16),
            pltpu.VMEM((NZ - 1, NH, QTR, *piece), BF16),
            pltpu.VMEM((NZ - 1, NH, QTR, *piece), BF16),
            pltpu.VMEM((QTR, NH, *piece), F32),
            pltpu.VMEM((QTR, *block), BF16),
            pltpu.VMEM((2 * hidden, hidden), F32),
            pltpu.VMEM((SLAB, height, hidden), F32),
            pltpu.VMEM((2, height, hidden), F32),
            pltpu.VMEM((NZ, height, hidden), F32),
            dma,
            dma((NZ,)),
            dma((NZ,)),
            dma((NZ,)),
            dma((NT,)),
            dma((NT,)),
            dma((NT, NY)),
            dma((NT, NY)),
            dma((NT, PEERS)),
            dma((NT, PEERS)),
            dma((NT,)),
            dma((NT, PEERS)),
            dma((NT, PEERS)),
            dma((NT, NY)),
            dma((NT, NY)),
            dma((NT,)),
            dma((NT,)),
            dma((2, NY)),
            dma((2, NY)),
            dma((SLAB,)),
            dma((SLAB,)),
            dma((NZ,)),
            dma((NZ,)),
            dma((SLAB,)),
            dma((SLAB,)),
        ],
        compiler_params=pltpu.CompilerParams(
            collective_id=0, has_side_effects=True, vmem_limit_bytes=VMEM_LIMIT
        ),
    )(etab, meta, nf, cot, wm, ws, adj)


def store_kernel(a_ref, b_ref, w_ref, oa_ref, ob_ref, om_ref, os_ref, sems):
    half = w_ref.shape[0] // 2
    copies = [
        pltpu.make_async_copy(src, dst, sems.at[i])
        for i, (src, dst) in enumerate(
            (
                (a_ref, oa_ref),
                (b_ref, ob_ref),
                (w_ref.at[pl.ds(0, half)], om_ref),
                (w_ref.at[pl.ds(half, half)], os_ref),
            )
        )
    ]
    for copy in copies:
        copy.start()
    for copy in copies:
        copy.wait()


def store(a, b, w):
    vmem = pl.BlockSpec(memory_space=pltpu.VMEM)
    hbm = pl.BlockSpec(memory_space=pl.ANY)
    piece = jax.ShapeDtypeStruct((w.shape[0] // 2, w.shape[1]), F32)
    return pl.pallas_call(
        store_kernel,
        name="store",
        out_shape=(
            jax.ShapeDtypeStruct(a.shape, a.dtype),
            jax.ShapeDtypeStruct(b.shape, b.dtype),
            piece,
            piece,
        ),
        in_specs=[vmem, vmem, vmem],
        out_specs=(hbm, hbm, hbm, hbm),
        scratch_shapes=[pltpu.SemaphoreType.DMA((4,))],
    )(a, b, w)


def by_slab(slots):
    rows = slots.reshape(NX, NZ, 2, 2).transpose(1, 0, 2, 3).reshape(NZ, CHUNK)
    return rows


def body(
    node_feat, cotangent, w_msg, w_self, adjacency, edge_src, edge_dst, send_src, recv_dst, live
):
    blocks = jnp.concatenate([by_slab(send_src), by_slab(recv_dst)], axis=0)
    blocks = jnp.pad(blocks, ((0, 0), (0, SLOTS - CHUNK)), constant_values=-1)
    slots = jnp.concatenate([edge_src.reshape(1, EDGES), edge_dst.reshape(1, EDGES)], axis=0)
    slots = jnp.pad(slots, ((0, 6), (0, SLOTS - EDGES)))
    row = lax.broadcasted_iota(I32, slots.shape, 0)
    slots = jnp.where(row == 2, live.reshape(1, 1), slots)
    meta, etab = tables(blocks, slots)
    adj = adjacency.reshape(-1, BLK, BLK)
    out, grad_feat, weights = layer(etab, meta, node_feat, cotangent, w_msg, w_self, adj)
    return store(out, grad_feat, weights)


def solution(mesh):
    in_specs = (
        P("edge", None),
        P("edge", None),
        P(),
        P(),
        P("edge", "feat", None, None, None),
        P("edge", "feat", None),
        P("edge", "feat", None),
        P("edge", "feat", None, None),
        P("edge", "feat", None, None),
        P("edge", "feat"),
    )
    out_specs = (P("edge", None), P("edge", None), P(), P())
    return jax.shard_map(body, mesh=mesh, in_specs=in_specs, out_specs=out_specs, check_vma=False)
```

```python
import jax
import jax.numpy as jnp
from jax import lax
from jax.experimental import pallas as pl
from jax.experimental.pallas import tpu as pltpu
from jax.sharding import PartitionSpec as P

MESH = pl.DeviceIdType.MESH
NX, NY, NZ = 4, 4, 8
BLK = 128
OWN = 16
QTR = OWN // NY
PEERS = 2 * NX
VMEM_LIMIT = 60 * 1024 * 1024
GROUP = 8
NH = 2
PIECE = BLK // NH
NT = NZ * NH
SLAB = NX * NY * 2
CHUNK = 2 * PEERS
EDGES = 64
SLOTS = 128
SRC, SRC_PREV, SRC_LAST, DST, DST_PREV, DST_LAST = range(6)
BF16, F32, I32 = jnp.bfloat16, jnp.float32, jnp.int32


def place():
    edge = lax.axis_index("edge")
    y = lax.axis_index("feat")
    return edge // 16, y, (edge // 2) % NZ, edge % 2


def device(x, y, z, c):
    return ((x * NZ + z) * 2 + c, y)


def zoff(k):
    return ((2 * (k % 2) - 1) * ((k + 1) // 2) + NZ) % NZ


def remote(src, dst, send, recv, peer):
    return pltpu.make_async_remote_copy(
        src_ref=src, dst_ref=dst, send_sem=send, recv_sem=recv, device_id=peer, device_id_type=MESH
    )


def slab_peer(x, c, j):
    return (x + j // 2) % NX, (c + j) % 2


def slab_source(x, c, j):
    return (x + NX - j // 2) % NX, (c + j) % 2


def slab_device(x, y, z, c, j):
    return device((x + j // (2 * NY)) % NX, (y + (j // 2) % NY) % NY, z, (c + j) % 2)


def loop(first, stop, body):
    def run(i, carry):
        body(i)
        return carry

    lax.fori_loop(first, stop, run, 0)


def dot(a, b, contract):
    return lax.dot_general(a, b, (contract, ((), ())), preferred_element_type=F32)


def tables_kernel(send_ref, recv_ref, src_ref, dst_ref, live_ref, meta_ref, etab_ref, pad):
    shape = pad.shape[1:]
    for s in range(2):
        pad[s] = jnp.zeros(shape, I32)
        pad[s, 0:1, 0:EDGES] = send_ref[s : s + 1, :]
        pad[s, 1:2, 0:EDGES] = recv_ref[s : s + 1, :]
    wide = (SLOTS, SLOTS)
    down = lax.broadcasted_iota(I32, wide, 0)
    along = lax.broadcasted_iota(I32, wide, 1)
    peer = (along % CHUNK) // 2
    edge = ((peer // 2) * NZ + along // CHUNK) * 2 + peer % 2
    found = jnp.zeros(shape, F32)
    for s in range(2):
        pick = jnp.where((down == edge) & (along % 2 == s), 1.0, 0.0).astype(BF16)
        found += dot(pad[s].astype(F32).astype(BF16), pick, ((1,), (0,)))
    blocks = found.astype(I32)
    spot = lax.broadcasted_iota(I32, shape, 1) % CHUNK
    prev = jnp.full(shape, CHUNK, I32)
    for d in range(CHUNK - 1, 0, -1):
        same = (pltpu.roll(blocks, d, 1) == blocks) & (spot >= d)
        prev = jnp.where(same, spot - d, prev)
    last = jnp.full(shape, -1, I32)
    for t in range(1 - CHUNK, CHUNK):
        other = blocks if t == 0 else pltpu.roll(blocks, (SLOTS - t) % SLOTS, 1)
        at = spot + t
        last = jnp.where((other == spot) & (at >= 0) & (at < CHUNK), at, last)
    last = jnp.where(last < 0, CHUNK, last)
    meta_ref[...] = jnp.zeros(shape, I32)
    for i in range(2):
        for row, value in enumerate((blocks, prev, last)):
            meta_ref[3 * i + row : 3 * i + row + 1] = value[i : i + 1]

    pad[0] = jnp.zeros(shape, I32)
    pad[0, 0:1, 0:EDGES] = src_ref[...]
    pad[0, 1:2, 0:EDGES] = dst_ref[...]
    downf, alongf = down.astype(F32), along.astype(F32)
    live = live_ref[0, 0]
    none = float(EDGES)
    for row, prev_row, last_row in ((0, SRC_PREV, SRC_LAST), (1, DST_PREV, DST_LAST)):
        slot = pad[0, row : row + 1, :]
        etab_ref[(SRC, DST)[row] : (SRC, DST)[row] + 1] = slot
        on = lax.broadcasted_iota(I32, slot.shape, 1) < live
        flat = jnp.where(on, slot.astype(F32), -1.0)
        tall = jnp.sum(jnp.where(down == along, flat, 0.0), axis=1, keepdims=True)
        before = jnp.where((tall == flat) & (down < along) & (tall >= 0.0), downf, -1.0)
        found = jnp.max(before, axis=0, keepdims=True)
        etab_ref[prev_row : prev_row + 1] = jnp.where(found < 0.0, none, found).astype(I32)
        ends = jnp.max(jnp.where(tall == alongf, downf, -1.0), axis=0, keepdims=True)
        etab_ref[last_row : last_row + 1] = jnp.where(ends < 0.0, none, ends).astype(I32)


def tables(send, recv, src, dst, live):
    vmem = pl.BlockSpec(memory_space=pltpu.VMEM)
    return pl.pallas_call(
        tables_kernel,
        name="tables",
        out_shape=(
            jax.ShapeDtypeStruct((8, SLOTS), I32),
            jax.ShapeDtypeStruct((8, SLOTS), I32),
        ),
        in_specs=[vmem, vmem, vmem, vmem, pl.BlockSpec(memory_space=pltpu.SMEM)],
        out_specs=(vmem, vmem),
        scratch_shapes=[pltpu.VMEM((2, 8, SLOTS), I32)],
    )(send, recv, src, dst, live)


def layer_kernel(
    etab_in, meta_ref, nf_in, cot_in, wm_in, ws_in, adj_in,
    out_ref, gf_ref, ow_ref,
    etab, nf_ref, cot_ref, wm_ref, ws_ref,
    meta_in, meta, adj, dense, chunk, staged, rows, chain, parts, arrived, runs,
    ysend, yown, yrecv, zsend, zrecv, total, pre, weights, first, mine, second,
    ins, ml, ms, mr, g_zs, g_zr, g_ys, g_yr, g_xs, g_xr,
    ls, s_xs, s_xr, s_ys, s_yr, s_zs, s_zr, gs, gr, s1, r1, s2, r2, s3, r3,
):
    x, y, z, c = place()
    me = x * 2 + c
    quarter = QTR * BLK
    here = device(x, y, z, c)
    mine_rows = pl.ds(quarter * y, quarter)
    own = pl.ds(QTR * y, QTR)

    fetches = [
        pltpu.make_async_copy(src, dst, ins.at[i])
        for i, (src, dst) in enumerate(
            (
                (nf_in, nf_ref),
                (wm_in, wm_ref),
                (ws_in, ws_ref),
                (cot_in.at[mine_rows], cot_ref),
                (etab_in, etab),
                (adj_in, adj),
            )
        )
    ]
    own_meta = pltpu.make_async_copy(meta_ref, meta.at[z], ml.at[0])
    for fetch in fetches[:2]:
        fetch.start()
    own_meta.start()
    barrier = pltpu.get_barrier_semaphore()
    peers = [slab_device(x, y, z, c, j) for j in range(1, SLAB)]
    peers += [device(x, y, (z + d) % NZ, c) for d in range(1, NZ)]
    for peer in peers:
        pl.semaphore_signal(barrier, inc=1, device_id=peer, device_id_type=MESH)
    for fetch in fetches[2:]:
        fetch.start()
    for fetch in fetches[:2]:
        fetch.wait()

    def project(i):
        b = (QTR * y + i) % OWN
        node = nf_ref[pl.ds(pl.multiple_of(b * BLK, BLK), BLK)]
        message = dot(node, wm_ref[...], ((1,), (0,))).astype(BF16)
        for h in range(NH):
            dense[z, h, b] = message[h * PIECE : (h + 1) * PIECE]

    loop(0, OWN, project)
    pl.semaphore_wait(barrier, len(peers))

    def slots_of(px, zi, pc):
        return pl.ds(((px * NZ + zi) * 2 + pc) * 2, 2)

    def gather(forward):
        block_row = SRC if forward else DST

        def source_of(t):
            return (z + NZ - zoff(t // NH)) % NZ

        def mcopy(d):
            return remote(
                meta_ref, meta_in.at[z], ms.at[d], mr.at[d],
                device(x, y, (z + d) % NZ, c),
            )

        def zcopy(zi, h, d, step):
            part = dense.at[zi, h, own]
            at = d * NH + h
            return remote(part, part, g_zs.at[at], g_zr.at[at], device(x, y, (z + NZ + step) % NZ, c))

        def ycopy(t, d):
            part = dense.at[source_of(t), t % NH, own]
            return remote(part, part, g_ys.at[t, d], g_yr.at[t, d], device(x, (y + d) % NY, z, c))

        def xcopy(t, j):
            px, pc = slab_peer(x, c, j)
            zi = source_of(t)
            return remote(
                staged.at[px * 2 + pc, zi, t % NH], rows.at[slots_of(x, zi, c), t % NH],
                g_xs.at[t, j], g_xr.at[t, j], device(px, y, z, pc),
            )

        def meta_load(k, zi):
            return pltpu.make_async_copy(meta_in.at[zi], meta.at[zi], ml.at[k])

        def spread(t):
            k, h = t // NH, t % NH
            d = zoff(k)
            zi = source_of(t)
            if forward:

                @pl.when(h == 0)
                def _():
                    remote(meta_ref, meta_in.at[zi], ms.at[d], mr.at[d], here).wait_recv()
                    meta_load(k, zi).start()

            part = dense.at[zi, h, own]
            at = d * NH + h
            remote(part, part, g_zs.at[at], g_zr.at[at], here).wait_recv()

            @pl.when(k < NZ - 2)
            def _():
                step = 2 * (k % 2) - 1
                zcopy(zi, h, (d + NZ + step) % NZ, step).start()

            for dy in (1, 3, 2):
                ycopy(t, dy).start()

        def collect(t):
            zi = source_of(t)
            for dy in (1, 3, 2):
                part = dense.at[zi, t % NH, pl.ds(QTR * ((y + NY - dy) % NY), QTR)]
                remote(part, part, g_ys.at[t, dy], g_yr.at[t, dy], here).wait_recv()
            if forward:

                @pl.when(t % NH == 0)
                def _():
                    meta_load(t // NH, zi).wait()

        def deliver(t):
            zi, h = source_of(t), t % NH
            chunk[...] = dense[zi, h]

            def pick(j):
                px, pc = slab_peer(x, c, j)
                pid = px * 2 + pc
                for s in range(2):
                    staged[pid, zi, h, s] = chunk[meta[zi, block_row, CHUNK * z + pid * 2 + s]]

            loop(1, PEERS, pick)
            base = ((x * NZ + zi) * 2 + c) * 2
            for s in range(2):
                rows[base + s, h] = chunk[meta[zi, block_row, CHUNK * z + me * 2 + s]]
            loop(1, PEERS, lambda j: xcopy(t, j).start())

        for h in range(NH):
            for d, step in ((1, 1), (NZ - 1, -1)):
                zcopy(z, h, d, step).start()
        if forward:
            for d in (1, 7, 2, 6, 3, 5, 4):
                mcopy(d).start()
            own_meta.wait()
            loop(0, NH, deliver)
            loop(NH, 2 * NH, spread)
        else:
            for h in range(NH):
                for dy in (1, 3, 2):
                    ycopy(h, dy).start()

        def step(t):
            @pl.when(t < NH * (NZ - 1))
            def _():
                spread(t + NH)

            collect(t)
            deliver(t)

        loop(NH if forward else 0, NH * NZ, step)

        for d in range(1, NZ):
            if forward:
                mcopy(d).wait_send()
            for h in range(NH):
                zcopy(z, h, d, 1).wait_send()

        def finish(t):
            zi = source_of(t)

            def each(j):
                xcopy(t, j).wait_send()
                sx, sc = slab_source(x, c, j)
                remote(
                    staged.at[me, zi, t % NH], rows.at[slots_of(sx, zi, sc), t % NH],
                    g_xs.at[t, j], g_xr.at[t, j], here,
                ).wait_recv()

            loop(1, PEERS, each)

        loop(0, NH * NZ, finish)

        def sent(t):
            for dy in range(1, NY):
                ycopy(t, dy).wait_send()

        loop(NH if forward else 0, NH * NZ, sent)

    def whole(pieces):
        return pieces.reshape(BLK, pieces.shape[-1])

    def edges(forward):
        pick, prev = (SRC, DST_PREV) if forward else (DST, SRC_PREV)
        contract = ((1,), (0,)) if forward else ((0,), (0,))
        chain[EDGES] = jnp.zeros(chain.shape[1:], F32)

        def one_round(r):
            terms = []
            for i in range(GROUP):
                k = r * GROUP + i
                terms.append(dot(adj[k], whole(rows[etab[pick, k]]), contract))
            for i in range(GROUP):
                k = r * GROUP + i
                chain[k] = terms[i].reshape(chain.shape[1:]) + chain[etab[prev, k]]

        loop(0, EDGES // GROUP, one_round)

    def scatter(forward):
        end = DST_LAST if forward else SRC_LAST
        run_prev, run_last = (DST_PREV, DST_LAST) if forward else (SRC_PREV, SRC_LAST)

        def owner(t):
            return (z + zoff(NZ - 1 - t // NH)) % NZ

        def xcopy(t, j):
            zi, h = owner(t), t % NH
            px, pc = slab_peer(x, c, j)
            return remote(
                parts.at[slots_of(px, zi, pc), h], arrived.at[zi, h, pl.ds(2 * me, 2)],
                s_xs.at[t, j], s_xr.at[t, j], device(px, y, z, pc),
            )

        def local(t):
            zi, h = owner(t), t % NH
            return pltpu.make_async_copy(
                parts.at[slots_of(x, zi, c), h], arrived.at[zi, h, pl.ds(2 * me, 2)], ls.at[t]
            )

        def ycopy(t, d):
            return remote(
                ysend.at[t, d - 1], yrecv.at[t, d - 1], s_ys.at[t, d], s_yr.at[t, d],
                device(x, (y + d) % NY, z, c),
            )

        def zcopy(d, h):
            at = d * NH + h
            return remote(
                zsend.at[d - 1, h], zrecv.at[d - 1, h], s_zs.at[at], s_zr.at[at],
                device(x, y, (z + d) % NZ, c),
            )

        def write(t):
            zi, h = owner(t), t % NH

            def each(pid):
                base = (((pid // 2) * NZ + zi) * 2 + pid % 2) * 2
                for s in range(2):
                    parts[base + s, h] = chain[etab[end, base + s], h].astype(BF16)

            loop(0, PEERS, each)

        def push(t):
            local(t).start()
            loop(1, PEERS, lambda j: xcopy(t, j).start())

        write(0)

        def issue(t):
            write(t)
            push(t - 1)

        loop(1, NH * NZ, issue)
        push(NH * NZ - 1)

        runs[CHUNK] = jnp.zeros(runs.shape[1:], F32)

        def merge(t):
            zi, h = owner(t), t % NH
            local(t).wait()

            def each(j):
                sx, sc = slab_source(x, c, j)
                remote(
                    parts.at[slots_of(x, zi, c), h], arrived.at[zi, h, pl.ds(2 * (sx * 2 + sc), 2)],
                    s_xs.at[t, j], s_xr.at[t, j], here,
                ).wait_recv()

            loop(1, PEERS, each)

            def run(i):
                runs[i] = arrived[zi, h, i].astype(F32) + runs[meta[zi, run_prev, CHUNK * z + i]]

            loop(0, CHUNK, run)
            for d in (1, 3, 2):
                base = QTR * ((y + d) % NY)
                for b in range(QTR):
                    ysend[t, d - 1, b] = runs[meta[zi, run_last, CHUNK * z + base + b]].astype(BF16)
                ycopy(t, d).start()
            for b in range(QTR):
                yown[t, b] = runs[meta[zi, run_last, CHUNK * z + QTR * y + b]]

        def total_of(t):
            for d in range(1, NY):
                ycopy(t, d).wait_recv()
            return [
                yown[t, b] + yrecv[t, 0, b].astype(F32) + yrecv[t, 1, b].astype(F32)
                + yrecv[t, 2, b].astype(F32)
                for b in range(QTR)
            ]

        def pass_on(t):
            d, h = zoff(NZ - 1 - t // NH), t % NH
            for b, value in enumerate(total_of(t)):
                zsend[d - 1, h, b] = value.astype(BF16)
            zcopy(d, h).start()

        loop(0, NH, merge)

        def step(t):
            merge(t)
            pass_on(t - NH)

        loop(NH, NH * NZ, step)
        for h in range(NH):
            for b, value in enumerate(total_of(NH * (NZ - 1) + h)):
                total[b, h] = value
        for d in (1, 7, 2, 6, 3, 5, 4):
            for h in range(NH):
                zcopy(d, h).wait_recv()
                for b in range(QTR):
                    total[b, h] += zrecv[d - 1, h, b].astype(F32)

        for d in range(1, NZ):
            for h in range(NH):
                zcopy(d, h).wait_send()

        def finish(t):
            for d in range(1, NY):
                ycopy(t, d).wait_send()
            loop(1, PEERS, lambda j: xcopy(t, j).wait_send())

        loop(0, NH * NZ, finish)

    def share(i, d):
        part = (out_ref, gf_ref)[i].at[mine_rows]
        return remote(part, part, gs.at[i, d], gr.at[i, d], device(x, (y + d) % NY, z, c))

    def shared(i):
        for d in range(1, NY):
            share(i, d).wait_send()
            part = (out_ref, gf_ref)[i].at[pl.ds(quarter * ((y + NY - d) % NY), quarter)]
            remote(part, part, gs.at[i, d], gr.at[i, d], here).wait_recv()

    def block_rows(b):
        return pl.ds(pl.multiple_of((QTR * y + b) * BLK, BLK), BLK)

    gather(True)
    for fetch in fetches[2:]:
        fetch.wait()
    edges(True)
    scatter(True)

    def activate(b):
        node = nf_ref[block_rows(b)]
        preact = dot(node, ws_ref[...], ((1,), (0,))) + whole(total[b])
        sig = jax.nn.sigmoid(preact)
        out_ref[block_rows(b)] = (preact * sig).astype(BF16)
        grad = cot_ref[BLK * b : BLK * (b + 1)].astype(F32) * sig * (1.0 + preact * (1.0 - sig))
        grad = grad.astype(BF16)
        pre[b] = grad
        for h in range(NH):
            dense[z, h, QTR * y + b] = grad[h * PIECE : (h + 1) * PIECE]

    def outer(at, b, value):
        term = dot(nf_ref[block_rows(b)], value, ((0,), (0,)))
        if b == 0:
            weights[at : at + BLK] = term
        else:
            weights[at : at + BLK] += term

    for b in range(QTR):
        activate(b)
    for b in range(QTR):
        outer(BLK, b, pre[b])

    gather(False)
    edges(False)
    for d in (1, 3, 2):
        share(0, d).start()
    scatter(False)

    for b in range(QTR):
        outer(0, b, whole(total[b]).astype(BF16))

    height = 2 * BLK // SLAB
    slab_me = (x * NY + y) * 2 + c

    def index(j):
        return (((x + j // (2 * NY)) % NX) * NY + (y + (j // 2) % NY) % NY) * 2 + (c + j) % 2

    def source(j):
        return (
            ((x + NX - j // (2 * NY)) % NX) * NY + (y + NY - (j // 2) % NY) % NY
        ) * 2 + (c + j) % 2

    def one(j):
        return remote(
            weights.at[pl.ds(height * index(j), height)], first.at[slab_me], s1.at[j], r1.at[j],
            slab_device(x, y, z, c, j),
        )

    def two(d):
        return remote(mine.at[0], second.at[z], s2.at[d], r2.at[d], device(x, y, (z + d) % NZ, c))

    def three(j):
        return remote(
            mine.at[1], ow_ref.at[pl.ds(height * slab_me, height)], s3.at[j], r3.at[j],
            slab_device(x, y, z, c, j),
        )

    loop(1, SLAB, lambda j: one(j).start())
    first[slab_me] = weights[pl.ds(height * slab_me, height)]
    for b in range(QTR):
        gf_ref[block_rows(b)] = (
            dot(pre[b], ws_ref[...], ((1,), (1,)))
            + dot(whole(total[b]).astype(BF16), wm_ref[...], ((1,), (1,)))
        ).astype(BF16)
    for d in (1, 3, 2):
        share(1, d).start()
    loop(
        1, SLAB,
        lambda j: remote(
            weights.at[pl.ds(0, height)], first.at[source(j)], s1.at[j], r1.at[j], here
        ).wait_recv(),
    )
    mine[0] = jnp.sum(first[...], axis=0)
    for d in range(1, NZ):
        two(d).start()
    second[z] = mine[0]
    for d in range(1, NZ):
        remote(mine.at[0], second.at[(z + NZ - d) % NZ], s2.at[d], r2.at[d], here).wait_recv()
    mine[1] = jnp.sum(second[...], axis=0)
    loop(1, SLAB, lambda j: three(j).start())
    ow_ref[pl.ds(height * slab_me, height)] = mine[1]
    loop(
        1, SLAB,
        lambda j: remote(
            mine.at[1], ow_ref.at[pl.ds(height * source(j), height)], s3.at[j], r3.at[j], here
        ).wait_recv(),
    )
    loop(1, SLAB, lambda j: one(j).wait_send())
    for d in range(1, NZ):
        two(d).wait_send()
    loop(1, SLAB, lambda j: three(j).wait_send())
    shared(0)
    shared(1)


def layer(etab, meta, nf, cot, wm, ws, adj):
    dma = pltpu.SemaphoreType.DMA
    vmem = pl.BlockSpec(memory_space=pltpu.VMEM)
    hidden = nf.shape[1]
    block, piece = (BLK, hidden), (PIECE, hidden)
    height = 2 * BLK // SLAB
    return pl.pallas_call(
        layer_kernel,
        name="layer",
        out_shape=(
            jax.ShapeDtypeStruct(nf.shape, BF16),
            jax.ShapeDtypeStruct(nf.shape, BF16),
            jax.ShapeDtypeStruct((2 * hidden, hidden), F32),
        ),
        in_specs=[pl.BlockSpec(memory_space=pl.ANY)] * 7,
        out_specs=(vmem, vmem, vmem),
        scratch_shapes=[
            pltpu.SMEM((8, SLOTS), I32),
            pltpu.VMEM(nf.shape, BF16),
            pltpu.VMEM((nf.shape[0] // NY, hidden), BF16),
            pltpu.VMEM(wm.shape, BF16),
            pltpu.VMEM(ws.shape, BF16),
            pltpu.VMEM((NZ, 8, SLOTS), I32),
            pltpu.SMEM((NZ, 8, SLOTS), I32),
            pltpu.VMEM((EDGES, BLK, BLK), BF16),
            pltpu.VMEM((NZ, NH, OWN, *piece), BF16),
            pltpu.VMEM((OWN, *piece), BF16),
            pltpu.VMEM((PEERS, NZ, NH, 2, *piece), BF16),
            pltpu.VMEM((SLOTS, NH, *piece), BF16),
            pltpu.VMEM((EDGES + 1, NH, *piece), F32),
            pltpu.VMEM((SLOTS, NH, *piece), BF16),
            pltpu.VMEM((NZ, NH, CHUNK, *piece), BF16),
            pltpu.VMEM((CHUNK + 1, *piece), F32),
            pltpu.VMEM((NT, NY - 1, QTR, *piece), BF16),
            pltpu.VMEM((NT, QTR, *piece), F32),
            pltpu.VMEM((NT, NY - 1, QTR, *piece), BF16),
            pltpu.VMEM((NZ - 1, NH, QTR, *piece), BF16),
            pltpu.VMEM((NZ - 1, NH, QTR, *piece), BF16),
            pltpu.VMEM((QTR, NH, *piece), F32),
            pltpu.VMEM((QTR, *block), BF16),
            pltpu.VMEM((2 * hidden, hidden), F32),
            pltpu.VMEM((SLAB, height, hidden), F32),
            pltpu.VMEM((2, height, hidden), F32),
            pltpu.VMEM((NZ, height, hidden), F32),
            dma((6,)),
            dma((NZ,)),
            dma((NZ,)),
            dma((NZ,)),
            dma((NT,)),
            dma((NT,)),
            dma((NT, NY)),
            dma((NT, NY)),
            dma((NT, PEERS)),
            dma((NT, PEERS)),
            dma((NT,)),
            dma((NT, PEERS)),
            dma((NT, PEERS)),
            dma((NT, NY)),
            dma((NT, NY)),
            dma((NT,)),
            dma((NT,)),
            dma((2, NY)),
            dma((2, NY)),
            dma((SLAB,)),
            dma((SLAB,)),
            dma((NZ,)),
            dma((NZ,)),
            dma((SLAB,)),
            dma((SLAB,)),
        ],
        compiler_params=pltpu.CompilerParams(
            collective_id=0, has_side_effects=True, vmem_limit_bytes=VMEM_LIMIT
        ),
    )(etab, meta, nf, cot, wm, ws, adj)


def store_kernel(a_ref, b_ref, w_ref, oa_ref, ob_ref, om_ref, os_ref, sems):
    half = w_ref.shape[0] // 2
    copies = [
        pltpu.make_async_copy(src, dst, sems.at[i])
        for i, (src, dst) in enumerate(
            (
                (a_ref, oa_ref),
                (b_ref, ob_ref),
                (w_ref.at[pl.ds(0, half)], om_ref),
                (w_ref.at[pl.ds(half, half)], os_ref),
            )
        )
    ]
    for copy in copies:
        copy.start()
    for copy in copies:
        copy.wait()


def store(a, b, w):
    vmem = pl.BlockSpec(memory_space=pltpu.VMEM)
    hbm = pl.BlockSpec(memory_space=pl.ANY)
    piece = jax.ShapeDtypeStruct((w.shape[0] // 2, w.shape[1]), F32)
    return pl.pallas_call(
        store_kernel,
        name="store",
        out_shape=(
            jax.ShapeDtypeStruct(a.shape, a.dtype),
            jax.ShapeDtypeStruct(b.shape, b.dtype),
            piece,
            piece,
        ),
        in_specs=[vmem, vmem, vmem],
        out_specs=(hbm, hbm, hbm, hbm),
        scratch_shapes=[pltpu.SemaphoreType.DMA((4,))],
    )(a, b, w)


def body(
    node_feat, cotangent, w_msg, w_self, adjacency, edge_src, edge_dst, send_src, recv_dst, live
):
    send, recv = send_src.reshape(-1, 2).T, recv_dst.reshape(-1, 2).T
    meta, etab = tables(send, recv, edge_src.reshape(1, -1), edge_dst.reshape(1, -1), live)
    adj = adjacency.reshape(-1, BLK, BLK)
    out, grad_feat, weights = layer(etab, meta, node_feat, cotangent, w_msg, w_self, adj)
    return store(out, grad_feat, weights)


def solution(mesh):
    in_specs = (
        P("edge", None),
        P("edge", None),
        P(),
        P(),
        P("edge", "feat", None, None, None),
        P("edge", "feat", None),
        P("edge", "feat", None),
        P("edge", "feat", None, None),
        P("edge", "feat", None, None),
        P("edge", "feat"),
    )
    out_specs = (P("edge", None), P("edge", None), P(), P())
    return jax.shard_map(body, mesh=mesh, in_specs=in_specs, out_specs=out_specs, check_vma=False)
```

```python
import jax
import jax.numpy as jnp
from jax import lax
from jax.experimental import pallas as pl
from jax.experimental.pallas import tpu as pltpu
from jax.sharding import PartitionSpec as P

MESH = pl.DeviceIdType.MESH
NX, NY, NZ = 4, 4, 8
BLK = 128
OWN = 16
QTR = OWN // NY
PEERS = 2 * NX
VMEM_LIMIT = 60 * 1024 * 1024
GROUP = 8
NH = 2
PIECE = BLK // NH
NT = NZ * NH
LEAD = 4
LAG = 4
SLAB = NX * NY * 2
CHUNK = 2 * PEERS
EDGES = 64
SLOTS = 128
SRC, SRC_PREV, SRC_LAST, DST, DST_PREV, DST_LAST = range(6)
BF16, F32, I32 = jnp.bfloat16, jnp.float32, jnp.int32


def place():
    edge = lax.axis_index("edge")
    y = lax.axis_index("feat")
    return edge // 16, y, (edge // 2) % NZ, edge % 2


def device(x, y, z, c):
    return ((x * NZ + z) * 2 + c, y)


def zoff(k):
    return ((2 * (k % 2) - 1) * ((k + 1) // 2) + NZ) % NZ


def remote(src, dst, send, recv, peer):
    return pltpu.make_async_remote_copy(
        src_ref=src, dst_ref=dst, send_sem=send, recv_sem=recv, device_id=peer, device_id_type=MESH
    )


def slab_peer(x, c, j):
    return (x + j // 2) % NX, (c + j) % 2


def slab_source(x, c, j):
    return (x + NX - j // 2) % NX, (c + j) % 2


def slab_device(x, y, z, c, j):
    return device((x + j // (2 * NY)) % NX, (y + (j // 2) % NY) % NY, z, (c + j) % 2)


def loop(first, stop, body):
    def run(i, carry):
        body(i)
        return carry

    lax.fori_loop(first, stop, run, 0)


def dot(a, b, contract):
    return lax.dot_general(a, b, (contract, ((), ())), preferred_element_type=F32)


def tables_kernel(send_ref, recv_ref, src_ref, dst_ref, live_ref, meta_ref, etab_ref, pad):
    shape = pad.shape[1:]
    for s in range(2):
        pad[s] = jnp.zeros(shape, I32)
        pad[s, 0:1, 0:EDGES] = send_ref[s : s + 1, :]
        pad[s, 1:2, 0:EDGES] = recv_ref[s : s + 1, :]
    wide = (SLOTS, SLOTS)
    down = lax.broadcasted_iota(I32, wide, 0)
    along = lax.broadcasted_iota(I32, wide, 1)
    peer = (along % CHUNK) // 2
    edge = ((peer // 2) * NZ + along // CHUNK) * 2 + peer % 2
    found = jnp.zeros(shape, F32)
    for s in range(2):
        pick = jnp.where((down == edge) & (along % 2 == s), 1.0, 0.0).astype(BF16)
        found += dot(pad[s].astype(F32).astype(BF16), pick, ((1,), (0,)))
    blocks = found.astype(I32)
    spot = lax.broadcasted_iota(I32, shape, 1) % CHUNK
    prev = jnp.full(shape, CHUNK, I32)
    for d in range(CHUNK - 1, 0, -1):
        same = (pltpu.roll(blocks, d, 1) == blocks) & (spot >= d)
        prev = jnp.where(same, spot - d, prev)
    last = jnp.full(shape, -1, I32)
    for t in range(1 - CHUNK, CHUNK):
        other = blocks if t == 0 else pltpu.roll(blocks, (SLOTS - t) % SLOTS, 1)
        at = spot + t
        last = jnp.where((other == spot) & (at >= 0) & (at < CHUNK), at, last)
    last = jnp.where(last < 0, CHUNK, last)
    meta_ref[...] = jnp.zeros(shape, I32)
    for i in range(2):
        for row, value in enumerate((blocks, prev, last)):
            meta_ref[3 * i + row : 3 * i + row + 1] = value[i : i + 1]

    pad[0] = jnp.zeros(shape, I32)
    pad[0, 0:1, 0:EDGES] = src_ref[...]
    pad[0, 1:2, 0:EDGES] = dst_ref[...]
    downf, alongf = down.astype(F32), along.astype(F32)
    live = live_ref[0, 0]
    none = float(EDGES)
    for row, prev_row, last_row in ((0, SRC_PREV, SRC_LAST), (1, DST_PREV, DST_LAST)):
        slot = pad[0, row : row + 1, :]
        etab_ref[(SRC, DST)[row] : (SRC, DST)[row] + 1] = (slot // 2) * (2 * NH) + slot % 2
        on = lax.broadcasted_iota(I32, slot.shape, 1) < live
        flat = jnp.where(on, slot.astype(F32), -1.0)
        tall = jnp.sum(jnp.where(down == along, flat, 0.0), axis=1, keepdims=True)
        before = jnp.where((tall == flat) & (down < along) & (tall >= 0.0), downf, -1.0)
        found = jnp.max(before, axis=0, keepdims=True)
        etab_ref[prev_row : prev_row + 1] = jnp.where(found < 0.0, none, found).astype(I32)
        ends = jnp.max(jnp.where(tall == alongf, downf, -1.0), axis=0, keepdims=True)
        etab_ref[last_row : last_row + 1] = jnp.where(ends < 0.0, none, ends).astype(I32)


def tables(send, recv, src, dst, live):
    vmem = pl.BlockSpec(memory_space=pltpu.VMEM)
    return pl.pallas_call(
        tables_kernel,
        name="tables",
        out_shape=(
            jax.ShapeDtypeStruct((8, SLOTS), I32),
            jax.ShapeDtypeStruct((8, SLOTS), I32),
        ),
        in_specs=[vmem, vmem, vmem, vmem, pl.BlockSpec(memory_space=pltpu.SMEM)],
        out_specs=(vmem, vmem),
        scratch_shapes=[pltpu.VMEM((2, 8, SLOTS), I32)],
    )(send, recv, src, dst, live)


def layer_kernel(
    etab_in, meta_ref, nf_in, cot_in, wm_in, ws_in, adj_in,
    out_ref, gf_ref, ow_ref,
    etab, nf_ref, cot_ref, wm_ref, ws_ref,
    meta_in, meta, adj, dense, chunk, staged, rows, chain, parts, arrived, runs,
    ysend, yown, yrecv, zsend, zrecv, total, pre, weights, first, mine, second,
    ins, ml, ms, mr, g_zs, g_zr, g_ys, g_yr, g_xs, g_xr,
    ls, s_xs, s_xr, s_ys, s_yr, s_zs, s_zr, gs, gr, s1, r1, s2, r2, s3, r3,
):
    x, y, z, c = place()
    me = x * 2 + c
    quarter = QTR * BLK
    here = device(x, y, z, c)
    mine_rows = pl.ds(quarter * y, quarter)
    own = pl.ds(QTR * y, QTR)

    fetches = [
        pltpu.make_async_copy(src, dst, ins.at[i])
        for i, (src, dst) in enumerate(
            (
                (nf_in, nf_ref),
                (wm_in, wm_ref),
                (ws_in, ws_ref),
                (cot_in.at[mine_rows], cot_ref),
                (etab_in, etab),
                (adj_in, adj),
            )
        )
    ]
    own_meta = pltpu.make_async_copy(meta_ref, meta.at[z], ml.at[0])
    for fetch in fetches[:2]:
        fetch.start()
    own_meta.start()
    barrier = pltpu.get_barrier_semaphore()
    peers = [slab_device(x, y, z, c, j) for j in range(1, SLAB)]
    peers += [device(x, y, (z + d) % NZ, c) for d in range(1, NZ)]
    for peer in peers:
        pl.semaphore_signal(barrier, inc=1, device_id=peer, device_id_type=MESH)
    for fetch in fetches[2:]:
        fetch.start()
    for fetch in fetches[:2]:
        fetch.wait()

    def project(i):
        b = (QTR * y + i) % OWN
        node = nf_ref[pl.ds(pl.multiple_of(b * BLK, BLK), BLK)]
        message = dot(node, wm_ref[...], ((1,), (0,))).astype(BF16)
        for h in range(NH):
            dense[z, h, b] = message[h * PIECE : (h + 1) * PIECE]

    loop(0, OWN, project)
    pl.semaphore_wait(barrier, len(peers))

    def spot_of(px, zi, pc, h):
        return (((px * NZ + zi) * 2 + pc) * NH + h) * 2

    def spots_of(px, zi, pc, h):
        return pl.ds(spot_of(px, zi, pc, h), 2)

    def gather(forward, after):
        block_row = SRC if forward else DST

        def source_of(t):
            return (z + NZ - zoff(t // NH)) % NZ

        def mcopy(d):
            return remote(
                meta_ref, meta_in.at[z], ms.at[d], mr.at[d],
                device(x, y, (z + d) % NZ, c),
            )

        def zcopy(zi, h, d, step):
            part = dense.at[zi, h, own]
            at = d * NH + h
            return remote(part, part, g_zs.at[at], g_zr.at[at], device(x, y, (z + NZ + step) % NZ, c))

        def ycopy(t, d):
            part = dense.at[source_of(t), t % NH, own]
            return remote(part, part, g_ys.at[t, d], g_yr.at[t, d], device(x, (y + d) % NY, z, c))

        def xcopy(t, j):
            px, pc = slab_peer(x, c, j)
            zi = source_of(t)
            return remote(
                staged.at[px * 2 + pc, zi, t % NH], rows.at[spots_of(x, zi, c, t % NH)],
                g_xs.at[t, j], g_xr.at[t, j], device(px, y, z, pc),
            )

        def meta_load(k, zi):
            return pltpu.make_async_copy(meta_in.at[zi], meta.at[zi], ml.at[k])

        def spread(t):
            k, h = t // NH, t % NH
            d = zoff(k)
            zi = source_of(t)
            if forward:

                @pl.when(h == 0)
                def _():
                    remote(meta_ref, meta_in.at[zi], ms.at[d], mr.at[d], here).wait_recv()
                    meta_load(k, zi).start()

            part = dense.at[zi, h, own]
            at = d * NH + h
            remote(part, part, g_zs.at[at], g_zr.at[at], here).wait_recv()

            @pl.when(k < NZ - 2)
            def _():
                step = 2 * (k % 2) - 1
                zcopy(zi, h, (d + NZ + step) % NZ, step).start()

            for dy in (1, 3, 2):
                ycopy(t, dy).start()

        def collect(t):
            zi = source_of(t)
            for dy in (1, 3, 2):
                part = dense.at[zi, t % NH, pl.ds(QTR * ((y + NY - dy) % NY), QTR)]
                remote(part, part, g_ys.at[t, dy], g_yr.at[t, dy], here).wait_recv()
            if forward:

                @pl.when(t % NH == 0)
                def _():
                    meta_load(t // NH, zi).wait()

        def deliver(t):
            zi, h = source_of(t), t % NH
            chunk[...] = dense[zi, h]

            def pick(j):
                px, pc = slab_peer(x, c, j)
                pid = px * 2 + pc
                for s in range(2):
                    staged[pid, zi, h, s] = chunk[meta[zi, block_row, CHUNK * z + pid * 2 + s]]

            loop(1, PEERS, pick)
            base = spot_of(x, zi, c, h)
            for s in range(2):
                rows[base + s] = chunk[meta[zi, block_row, CHUNK * z + me * 2 + s]]
            loop(1, PEERS, lambda j: xcopy(t, j).start())

        for h in range(NH):
            for d, step in ((1, 1), (NZ - 1, -1)):
                zcopy(z, h, d, step).start()
        if forward:
            for d in (1, 7, 2, 6, 3, 5, 4):
                mcopy(d).start()
            own_meta.wait()
            loop(0, NH, deliver)
            loop(NH, 2 * NH, spread)
        else:
            for h in range(NH):
                for dy in (1, 3, 2):
                    ycopy(h, dy).start()

        def drain(t):
            zi = source_of(t)

            def each(j):
                xcopy(t, j).wait_send()
                sx, sc = slab_source(x, c, j)
                remote(
                    staged.at[me, zi, t % NH], rows.at[spots_of(sx, zi, sc, t % NH)],
                    g_xs.at[t, j], g_xr.at[t, j], here,
                ).wait_recv()

            loop(1, PEERS, each)

        def step(t):
            @pl.when(t < NH * (NZ - 1))
            def _():
                spread(t + NH)

            collect(t)
            deliver(t)

            @pl.when(t >= LAG)
            def _():
                drain(t - LAG)
                if forward:

                    @pl.when(t >= LAG + NH)
                    def _():
                        for dy in range(1, NY):
                            ycopy(t - LAG, dy).wait_send()
                else:
                    for dy in range(1, NY):
                        ycopy(t - LAG, dy).wait_send()

        loop(NH if forward else 0, NT, step)
        after()

        for d in range(1, NZ):
            if forward:
                mcopy(d).wait_send()
            for h in range(NH):
                zcopy(z, h, d, 1).wait_send()

        def rest(t):
            drain(t)
            for dy in range(1, NY):
                ycopy(t, dy).wait_send()

        loop(NT - LAG, NT, rest)

    def whole(pieces):
        return pieces.reshape(BLK, pieces.shape[-1])

    def edges(forward):
        pick, prev = (SRC, DST_PREV) if forward else (DST, SRC_PREV)
        contract = ((1,), (0,)) if forward else ((0,), (0,))
        chain[EDGES] = jnp.zeros(chain.shape[1:], F32)

        def one_round(r):
            terms = []
            for i in range(GROUP):
                k = r * GROUP + i
                at = etab[pick, k]
                block = jnp.concatenate([rows[at + 2 * h] for h in range(NH)], axis=0)
                terms.append(dot(adj[k], block, contract))
            for i in range(GROUP):
                k = r * GROUP + i
                chain[k] = terms[i].reshape(chain.shape[1:]) + chain[etab[prev, k]]

        loop(0, EDGES // GROUP, one_round)

    def scatter(forward):
        end = DST_LAST if forward else SRC_LAST
        run_prev, run_last = (DST_PREV, DST_LAST) if forward else (SRC_PREV, SRC_LAST)

        def owner(t):
            return (z + zoff(NZ - 1 - t // NH)) % NZ

        def xcopy(t, j):
            zi, h = owner(t), t % NH
            px, pc = slab_peer(x, c, j)
            return remote(
                parts.at[spots_of(px, zi, pc, h)], arrived.at[zi, h, pl.ds(2 * me, 2)],
                s_xs.at[t, j], s_xr.at[t, j], device(px, y, z, pc),
            )

        def local(t):
            zi, h = owner(t), t % NH
            return pltpu.make_async_copy(
                parts.at[spots_of(x, zi, c, h)], arrived.at[zi, h, pl.ds(2 * me, 2)], ls.at[t]
            )

        def ycopy(t, d):
            return remote(
                ysend.at[t, d - 1], yrecv.at[t, d - 1], s_ys.at[t, d], s_yr.at[t, d],
                device(x, (y + d) % NY, z, c),
            )

        def zcopy(d, h):
            at = d * NH + h
            return remote(
                zsend.at[d - 1, h], zrecv.at[d - 1, h], s_zs.at[at], s_zr.at[at],
                device(x, y, (z + d) % NZ, c),
            )

        def write(t):
            zi, h = owner(t), t % NH

            def each(pid):
                base = (((pid // 2) * NZ + zi) * 2 + pid % 2) * 2
                to = spot_of(pid // 2, zi, pid % 2, h)
                for s in range(2):
                    parts[to + s] = chain[etab[end, base + s], h].astype(BF16)

            loop(0, PEERS, each)

        def push(t):
            local(t).start()
            loop(1, PEERS, lambda j: xcopy(t, j).start())

        write(0)

        def issue(t):
            write(t)
            push(t - 1)

        loop(1, LEAD + 1, issue)

        runs[CHUNK] = jnp.zeros(runs.shape[1:], F32)

        def merge(t):
            zi, h = owner(t), t % NH
            local(t).wait()

            def each(j):
                sx, sc = slab_source(x, c, j)
                remote(
                    parts.at[spots_of(x, zi, c, h)], arrived.at[zi, h, pl.ds(2 * (sx * 2 + sc), 2)],
                    s_xs.at[t, j], s_xr.at[t, j], here,
                ).wait_recv()

            loop(1, PEERS, each)

            def run(i):
                runs[i] = arrived[zi, h, i].astype(F32) + runs[meta[zi, run_prev, CHUNK * z + i]]

            loop(0, CHUNK, run)
            for d in (1, 3, 2):
                base = QTR * ((y + d) % NY)
                for b in range(QTR):
                    ysend[t, d - 1, b] = runs[meta[zi, run_last, CHUNK * z + base + b]].astype(BF16)
                ycopy(t, d).start()
            for b in range(QTR):
                yown[t, b] = runs[meta[zi, run_last, CHUNK * z + QTR * y + b]]

        def total_of(t):
            for d in range(1, NY):
                ycopy(t, d).wait_recv()
            return [
                yown[t, b] + yrecv[t, 0, b].astype(F32) + yrecv[t, 1, b].astype(F32)
                + yrecv[t, 2, b].astype(F32)
                for b in range(QTR)
            ]

        def pass_on(t):
            d, h = zoff(NZ - 1 - t // NH), t % NH
            for b, value in enumerate(total_of(t)):
                zsend[d - 1, h, b] = value.astype(BF16)
            zcopy(d, h).start()

        def drain(t):
            for d in range(1, NY):
                ycopy(t, d).wait_send()
            loop(1, PEERS, lambda j: xcopy(t, j).wait_send())

        def step(t):
            merge(t)

            @pl.when(t < NT - LEAD - 1)
            def _():
                write(t + LEAD + 1)

            @pl.when(t < NT - LEAD)
            def _():
                push(t + LEAD)

            @pl.when(t >= NH)
            def _():
                pass_on(t - NH)

            @pl.when(t >= LAG)
            def _():
                drain(t - LAG)

        loop(0, NT, step)
        for h in range(NH):
            for b, value in enumerate(total_of(NH * (NZ - 1) + h)):
                total[b, h] = value
        for d in (1, 7, 2, 6, 3, 5, 4):
            for h in range(NH):
                zcopy(d, h).wait_recv()
                for b in range(QTR):
                    total[b, h] += zrecv[d - 1, h, b].astype(F32)

        for d in range(1, NZ):
            for h in range(NH):
                zcopy(d, h).wait_send()

        loop(NT - LAG, NT, drain)

    def share(i, d):
        part = (out_ref, gf_ref)[i].at[mine_rows]
        return remote(part, part, gs.at[i, d], gr.at[i, d], device(x, (y + d) % NY, z, c))

    def shared(i):
        for d in range(1, NY):
            share(i, d).wait_send()
            part = (out_ref, gf_ref)[i].at[pl.ds(quarter * ((y + NY - d) % NY), quarter)]
            remote(part, part, gs.at[i, d], gr.at[i, d], here).wait_recv()

    def block_rows(b):
        return pl.ds(pl.multiple_of((QTR * y + b) * BLK, BLK), BLK)

    gather(True, lambda: None)
    for fetch in fetches[2:]:
        fetch.wait()
    edges(True)
    scatter(True)

    def activate(b):
        node = nf_ref[block_rows(b)]
        preact = dot(node, ws_ref[...], ((1,), (0,))) + whole(total[b])
        sig = jax.nn.sigmoid(preact)
        out_ref[block_rows(b)] = (preact * sig).astype(BF16)
        grad = cot_ref[BLK * b : BLK * (b + 1)].astype(F32) * sig * (1.0 + preact * (1.0 - sig))
        grad = grad.astype(BF16)
        pre[b] = grad
        for h in range(NH):
            dense[z, h, QTR * y + b] = grad[h * PIECE : (h + 1) * PIECE]

    def outer(at, b, value):
        term = dot(nf_ref[block_rows(b)], value, ((0,), (0,)))
        if b == 0:
            weights[at : at + BLK] = term
        else:
            weights[at : at + BLK] += term

    for b in range(QTR):
        activate(b)
    for b in range(QTR):
        outer(BLK, b, pre[b])

    def share_out():
        for d in (1, 3, 2):
            share(0, d).start()

    gather(False, share_out)
    edges(False)
    scatter(False)

    for b in range(QTR):
        outer(0, b, whole(total[b]).astype(BF16))

    height = 2 * BLK // SLAB
    slab_me = (x * NY + y) * 2 + c

    def index(j):
        return (((x + j // (2 * NY)) % NX) * NY + (y + (j // 2) % NY) % NY) * 2 + (c + j) % 2

    def source(j):
        return (
            ((x + NX - j // (2 * NY)) % NX) * NY + (y + NY - (j // 2) % NY) % NY
        ) * 2 + (c + j) % 2

    def one(j):
        return remote(
            weights.at[pl.ds(height * index(j), height)], first.at[slab_me], s1.at[j], r1.at[j],
            slab_device(x, y, z, c, j),
        )

    def two(d):
        return remote(mine.at[0], second.at[z], s2.at[d], r2.at[d], device(x, y, (z + d) % NZ, c))

    def three(j):
        return remote(
            mine.at[1], ow_ref.at[pl.ds(height * slab_me, height)], s3.at[j], r3.at[j],
            slab_device(x, y, z, c, j),
        )

    loop(1, SLAB, lambda j: one(j).start())
    first[slab_me] = weights[pl.ds(height * slab_me, height)]
    for b in range(QTR):
        gf_ref[block_rows(b)] = (
            dot(pre[b], ws_ref[...], ((1,), (1,)))
            + dot(whole(total[b]).astype(BF16), wm_ref[...], ((1,), (1,)))
        ).astype(BF16)
    for d in (1, 3, 2):
        share(1, d).start()
    loop(
        1, SLAB,
        lambda j: remote(
            weights.at[pl.ds(0, height)], first.at[source(j)], s1.at[j], r1.at[j], here
        ).wait_recv(),
    )
    mine[0] = jnp.sum(first[...], axis=0)
    for d in range(1, NZ):
        two(d).start()
    second[z] = mine[0]
    for d in range(1, NZ):
        remote(mine.at[0], second.at[(z + NZ - d) % NZ], s2.at[d], r2.at[d], here).wait_recv()
    mine[1] = jnp.sum(second[...], axis=0)
    loop(1, SLAB, lambda j: three(j).start())
    ow_ref[pl.ds(height * slab_me, height)] = mine[1]
    loop(
        1, SLAB,
        lambda j: remote(
            mine.at[1], ow_ref.at[pl.ds(height * source(j), height)], s3.at[j], r3.at[j], here
        ).wait_recv(),
    )
    loop(1, SLAB, lambda j: one(j).wait_send())
    for d in range(1, NZ):
        two(d).wait_send()
    loop(1, SLAB, lambda j: three(j).wait_send())
    shared(0)
    shared(1)


def layer(etab, meta, nf, cot, wm, ws, adj):
    dma = pltpu.SemaphoreType.DMA
    vmem = pl.BlockSpec(memory_space=pltpu.VMEM)
    hidden = nf.shape[1]
    block, piece = (BLK, hidden), (PIECE, hidden)
    height = 2 * BLK // SLAB
    return pl.pallas_call(
        layer_kernel,
        name="layer",
        out_shape=(
            jax.ShapeDtypeStruct(nf.shape, BF16),
            jax.ShapeDtypeStruct(nf.shape, BF16),
            jax.ShapeDtypeStruct((2 * hidden, hidden), F32),
        ),
        in_specs=[pl.BlockSpec(memory_space=pl.ANY)] * 7,
        out_specs=(vmem, vmem, vmem),
        scratch_shapes=[
            pltpu.SMEM((8, SLOTS), I32),
            pltpu.VMEM(nf.shape, BF16),
            pltpu.VMEM((nf.shape[0] // NY, hidden), BF16),
            pltpu.VMEM(wm.shape, BF16),
            pltpu.VMEM(ws.shape, BF16),
            pltpu.VMEM((NZ, 8, SLOTS), I32),
            pltpu.SMEM((NZ, 8, SLOTS), I32),
            pltpu.VMEM((EDGES, BLK, BLK), BF16),
            pltpu.VMEM((NZ, NH, OWN, *piece), BF16),
            pltpu.VMEM((OWN, *piece), BF16),
            pltpu.VMEM((PEERS, NZ, NH, 2, *piece), BF16),
            pltpu.VMEM((SLOTS * NH, *piece), BF16),
            pltpu.VMEM((EDGES + 1, NH, *piece), F32),
            pltpu.VMEM((SLOTS * NH, *piece), BF16),
            pltpu.VMEM((NZ, NH, CHUNK, *piece), BF16),
            pltpu.VMEM((CHUNK + 1, *piece), F32),
            pltpu.VMEM((NT, NY - 1, QTR, *piece), BF16),
            pltpu.VMEM((NT, QTR, *piece), F32),
            pltpu.VMEM((NT, NY - 1, QTR, *piece), BF16),
            pltpu.VMEM((NZ - 1, NH, QTR, *piece), BF16),
            pltpu.VMEM((NZ - 1, NH, QTR, *piece), BF16),
            pltpu.VMEM((QTR, NH, *piece), F32),
            pltpu.VMEM((QTR, *block), BF16),
            pltpu.VMEM((2 * hidden, hidden), F32),
            pltpu.VMEM((SLAB, height, hidden), F32),
            pltpu.VMEM((2, height, hidden), F32),
            pltpu.VMEM((NZ, height, hidden), F32),
            dma((6,)),
            dma((NZ,)),
            dma((NZ,)),
            dma((NZ,)),
            dma((NT,)),
            dma((NT,)),
            dma((NT, NY)),
            dma((NT, NY)),
            dma((NT, PEERS)),
            dma((NT, PEERS)),
            dma((NT,)),
            dma((NT, PEERS)),
            dma((NT, PEERS)),
            dma((NT, NY)),
            dma((NT, NY)),
            dma((NT,)),
            dma((NT,)),
            dma((2, NY)),
            dma((2, NY)),
            dma((SLAB,)),
            dma((SLAB,)),
            dma((NZ,)),
            dma((NZ,)),
            dma((SLAB,)),
            dma((SLAB,)),
        ],
        compiler_params=pltpu.CompilerParams(
            collective_id=0, has_side_effects=True, vmem_limit_bytes=VMEM_LIMIT
        ),
    )(etab, meta, nf, cot, wm, ws, adj)


def store_kernel(a_ref, b_ref, w_ref, oa_ref, ob_ref, om_ref, os_ref, sems):
    half = w_ref.shape[0] // 2
    copies = [
        pltpu.make_async_copy(src, dst, sems.at[i])
        for i, (src, dst) in enumerate(
            (
                (a_ref, oa_ref),
                (b_ref, ob_ref),
                (w_ref.at[pl.ds(0, half)], om_ref),
                (w_ref.at[pl.ds(half, half)], os_ref),
            )
        )
    ]
    for copy in copies:
        copy.start()
    for copy in copies:
        copy.wait()


def store(a, b, w):
    vmem = pl.BlockSpec(memory_space=pltpu.VMEM)
    hbm = pl.BlockSpec(memory_space=pl.ANY)
    piece = jax.ShapeDtypeStruct((w.shape[0] // 2, w.shape[1]), F32)
    return pl.pallas_call(
        store_kernel,
        name="store",
        out_shape=(
            jax.ShapeDtypeStruct(a.shape, a.dtype),
            jax.ShapeDtypeStruct(b.shape, b.dtype),
            piece,
            piece,
        ),
        in_specs=[vmem, vmem, vmem],
        out_specs=(hbm, hbm, hbm, hbm),
        scratch_shapes=[pltpu.SemaphoreType.DMA((4,))],
    )(a, b, w)


def body(
    node_feat, cotangent, w_msg, w_self, adjacency, edge_src, edge_dst, send_src, recv_dst, live
):
    send, recv = send_src.reshape(-1, 2).T, recv_dst.reshape(-1, 2).T
    meta, etab = tables(send, recv, edge_src.reshape(1, -1), edge_dst.reshape(1, -1), live)
    adj = adjacency.reshape(-1, BLK, BLK)
    out, grad_feat, weights = layer(etab, meta, node_feat, cotangent, w_msg, w_self, adj)
    return store(out, grad_feat, weights)


def solution(mesh):
    in_specs = (
        P("edge", None),
        P("edge", None),
        P(),
        P(),
        P("edge", "feat", None, None, None),
        P("edge", "feat", None),
        P("edge", "feat", None),
        P("edge", "feat", None, None),
        P("edge", "feat", None, None),
        P("edge", "feat"),
    )
    out_specs = (P("edge", None), P("edge", None), P(), P())
    return jax.shard_map(body, mesh=mesh, in_specs=in_specs, out_specs=out_specs, check_vma=False)
```
